512 devices in a mesh: src: 16 (over z, x_lo), xl: 32 (over y, x_hi, core).
Axes of the slice: x: 4 (x_hi: 2, x_lo: 2; x = x_hi * 2 + x_lo), y: 8, z: 8, core: 2. Of those that a mesh axis runs over, the one named last changes fastest.
Arguments:
- src_traces: float32 [256, 1024, 1024], P('src', 'xl'), may hold values from -6 to 6
- rec_traces: float32 [1024, 256, 1024], P('xl', 'src'), may hold values from -6 to 6
Outputs:
- multiples: float32 [256, 256, 256], P('src', 'xl')
The draws below stay inside these ranges and needn't reach their ends.
All inputs are finite; a program needn't handle non-finite values.
Results may differ from the reference program's by a relative error of at most 0.004.
Values may be sent and summed in bfloat16 or wider, within the bound.
A program may use at most 64 MiB of HBM per device.

```python
import math
import jax
import jax.numpy as jnp
from jax import lax

NT = 1024
F = 128
FBASE = 4
S = 256
XPTS = 1024
RCV = 256


def raised(values, stream_key, source, target, shards_of, factor):
    def block_of(axis_at):
        return (jnp.arange(values.shape[axis_at]) // (values.shape[axis_at] // shards_of)).reshape((-1,) + (1,) * (values.ndim - 1 - axis_at))

    one_side = jax.random.permutation(stream_key, shards_of)[block_of(target)]
    second = (block_of(target) + shards_of // 2) % shards_of
    return jnp.where((block_of(source) == one_side) | (block_of(source) == second), factor * values, values)


def block_scale(stream_key, shape, split, least, top_value):
    loudness, own = 1.0, jax.random.fold_in(stream_key, 6)
    for axis_at, shards_of in split:
        draws = jnp.exp(jax.random.uniform(jax.random.fold_in(own, axis_at), (shards_of,), jnp.float32, least / len(split), top_value / len(split)))
        loudness = loudness * jnp.repeat(draws, shape[axis_at] // shards_of).reshape([-1 if axis == axis_at else 1 for axis in range(len(shape))])
    return loudness


def gaussian(rng, dims, scale, reach, cuts=(), held_as=jnp.bfloat16):
    entries = scale * jax.random.normal(rng, dims, jnp.float32)
    if cuts:
        entries = entries * block_scale(rng, dims, cuts, -0.22, 0.18)
    return jnp.clip(entries, -reach, reach).astype(held_as)


def heavy_noise(stream_key, extent, scale, most, cuts, heavy, kind=jnp.bfloat16):
    array = scale * jax.random.normal(stream_key, extent, jnp.float32)
    if cuts:
        array = array * block_scale(stream_key, extent, cuts, -0.22, 0.18)
    return jnp.clip(raised(array, jax.random.fold_in(stream_key, 3), *heavy), -most, most).astype(kind)


def setup_inputs(seed: int = 0) -> dict:
    splits = jax.random.split(jax.random.key(seed), 3)
    src_traces = gaussian(splits[0], (S, XPTS, NT), 1.0, 6.0, ((0, 16), (1, 32)), jnp.float32)
    rec_traces = heavy_noise(splits[1], (XPTS, RCV, NT), 1.0, 6.0, ((0, 32), (1, 16)), (0, 1, 32, 2.75), jnp.float32)
    return dict(src_traces=src_traces, rec_traces=rec_traces)


def fourier_table(samples):
    times = jnp.arange(samples, dtype=jnp.int32)
    freq_bins = FBASE + jnp.arange(F, dtype=jnp.int32)
    phases = times[:, None] * freq_bins[None, :] % samples
    angles = phases.astype(jnp.float32) * jnp.float32(2.0 * math.pi / samples)
    basis = jnp.concatenate([jnp.cos(angles), -jnp.sin(angles)], axis=1)
    return basis / jnp.float32(math.sqrt(samples))

def spectra(traces):
    samples = traces.shape[-1]
    flat_rows = traces.reshape(-1, samples)
    result = jnp.dot(flat_rows, fourier_table(samples), precision=lax.Precision.HIGHEST, preferred_element_type=jnp.float32)
    return result.reshape(traces.shape[:-1] + (2 * F,)).astype(jnp.bfloat16)

def spectral_product(left, right):
    left_re = left[..., :F].astype(jnp.float32)
    left_im = left[..., F:].astype(jnp.float32)
    right_re = right[..., :F].astype(jnp.float32)
    right_im = right[..., F:].astype(jnp.float32)
    layout_kind = 'ltu,teu->leu'
    real_part = jnp.einsum(layout_kind, left_re, right_re) - jnp.einsum(layout_kind, left_im, right_im)
    imag_part = jnp.einsum(layout_kind, left_re, right_im) + jnp.einsum(layout_kind, left_im, right_re)
    return jnp.concatenate([real_part, imag_part], axis=-1)

def reference(src_traces, rec_traces):
    shot_source = spectra(src_traces)
    panels = spectra(rec_traces)
    return spectral_product(shot_source, panels) * jnp.float32(1.0 / math.sqrt(XPTS))
```

```python
import math

import jax
import jax.numpy as jnp
from jax import lax
from jax.sharding import PartitionSpec as P

F = 128
FBASE = 4
Y = 8
Q = 4


def fourier_table(samples):
    times = jnp.arange(samples, dtype=jnp.int32)
    freq_bins = FBASE + jnp.arange(F, dtype=jnp.int32)
    phases = times[:, None] * freq_bins[None, :] % samples
    angles = phases.astype(jnp.float32) * jnp.float32(2.0 * math.pi / samples)
    basis = jnp.concatenate([jnp.cos(angles), -jnp.sin(angles)], axis=1)
    return basis / jnp.float32(math.sqrt(samples))


def spectra(traces):
    samples = traces.shape[-1]
    rows = traces.reshape(-1, samples)
    out = lax.dot_general(
        fourier_table(samples), rows, (((0,), (1,)), ((), ())),
        precision=lax.Precision.HIGHEST, preferred_element_type=jnp.float32)
    return out.astype(jnp.bfloat16)


def per_device(src_traces, rec_traces):
    ns = lax.axis_size("src")
    ygroups = [[y * Q + q for y in range(Y)] for q in range(Q)]
    qgroups = [[y * Q + q for q in range(Q)] for y in range(Y)]
    s, x = src_traces.shape[:2]
    r = rec_traces.shape[1]
    weight = jnp.float32(1.0 / math.sqrt(x * Y * Q))

    def spread(traces):
        spec = spectra(traces)
        spec = spec.reshape(2, ns, Y, -1).transpose(1, 2, 0, 3)
        spec = lax.all_to_all(spec, "src", 0, 0)
        return lax.all_to_all(spec, "xl", 1, 0, axis_index_groups=ygroups)

    b = spread(rec_traces).reshape(Y, ns, 2, x, r)
    a = spread(src_traces).reshape(Y, ns, 2, s, x)
    b = b.transpose(2, 0, 3, 1, 4).reshape(2, Y * x, ns * r)
    a = a.transpose(2, 1, 3, 0, 4).reshape(2, ns * s, Y * x)

    def dot(u, v):
        return jnp.dot(u, v, preferred_element_type=jnp.float32)

    re = dot(a[0], b[0]) - dot(a[1], b[1])
    im = dot(a[0], b[1]) + dot(a[1], b[0])
    c = jnp.stack([re, im]) * weight
    c = c.reshape(2, ns, s, Y, Q, -1).transpose(4, 3, 1, 0, 2, 5)
    c = lax.psum_scatter(c, "xl", scatter_dimension=0, axis_index_groups=qgroups)
    c = lax.all_to_all(c, "xl", 0, 0, axis_index_groups=ygroups)
    c = lax.all_to_all(c, "src", 1, 0)
    c = c.transpose(3, 4, 2, 0, 1)
    return c.reshape(s, -1, 2 * F)


def solution(mesh):
    return jax.shard_map(
        per_device,
        mesh=mesh,
        in_specs=(P("src", "xl", None), P("xl", "src", None)),
        out_specs=P("src", "xl", None),
        check_vma=False,
    )
```

```python
import functools
import math

import jax
import jax.numpy as jnp
import numpy as np
from jax import lax
from jax.experimental import pallas as pl
from jax.experimental.pallas import tpu as pltpu
from jax.sharding import PartitionSpec as P

F = 128
FBASE = 4
Q = 4
BF = jnp.bfloat16
F32 = jnp.float32
MESH = pl.DeviceIdType.MESH
NT = (((1,), (1,)), ((), ()))


def fourier_parts(samples):
    times = np.arange(samples, dtype=np.int64)
    bins = FBASE + np.arange(F, dtype=np.int64)
    angles = (bins[:, None] * times[None, :] % samples) * (2.0 * math.pi / samples)
    table = np.concatenate([np.cos(angles), -np.sin(angles)], axis=0) / math.sqrt(samples)
    table = table.astype(np.float32)
    high = table.astype(jnp.bfloat16)
    low = (table - high.astype(np.float32)).astype(jnp.bfloat16)
    return high, low


def dot_nt(a, b):
    return lax.dot_general(a, b, NT, preferred_element_type=F32)


def lane_bit(shape, bit):
    lanes = lax.broadcasted_iota(jnp.int32, shape, len(shape) - 1)
    return ((lanes >> bit) & 1) == 0


def kernel(ns, ny, scale, src_ref, rec_ref, thi_ref, tlo_ref, out_ref,
           xa, xb, th, tl, xh, xlo, u, s_buf, r1, r2, acat, bb,
           psend, precv, cown, xsend, xrecv, ck, d_buf, e_buf, t_buf, h_buf, g_buf,
           in_sem, s1_send, s1_recv, s2_send, s2_recv, loc_sem, p_sem, x_sem,
           c1_send, c1_recv, c2_send, c2_recv):
    me = lax.axis_index("src")
    j = lax.axis_index("xl")
    my_y = j // Q
    q = j % Q
    m = j // 2
    c = j % 2
    hi = m % 2
    nm = 2 * ny

    def load(a, b, k):
        return pltpu.make_async_copy(a, b, in_sem.at[k])

    loads = [load(thi_ref, th, 0), load(tlo_ref, tl, 1), load(src_ref, xa, 2)]
    rec_loads = [load(rec_ref.at[:, pl.ds(t * 128, 128)], xb.at[t], 3 + t) for t in range(8)]
    for item in loads + rec_loads:
        item.start()

    barrier = pltpu.get_barrier_semaphore()

    def greet_src(k, carry):
        pl.semaphore_signal(barrier, inc=1, device_id={"src": (me + k) % ns, "xl": j}, device_id_type=MESH)
        return carry

    def greet_m(k, carry):
        pl.semaphore_signal(barrier, inc=1, device_id={"src": me, "xl": ((m + k) % nm) * 2 + c}, device_id_type=MESH)
        return carry

    lax.fori_loop(1, ns, greet_src, 0)
    lax.fori_loop(1, nm, greet_m, 0)
    pl.semaphore_signal(barrier, inc=1, device_id={"src": me, "xl": m * 2 + 1 - c}, device_id_type=MESH)

    for item in loads:
        item.wait()

    def split(rows, start):
        high = rows.astype(BF)
        xh[pl.ds(start, rows.shape[0]), :] = high
        xlo[pl.ds(start, rows.shape[0]), :] = (rows - high.astype(F32)).astype(BF)

    def split_a(k, carry):
        at = pl.multiple_of(k * 64, 64)
        split(xa[pl.ds(at, 64), :], at)
        return carry

    def split_b(r, carry):
        slot = (r % 8) // 2 * 4 + (r // 8) * 2 + r % 2
        rows = jnp.concatenate([xb[t, pl.ds(r, 32, stride=16), :] for t in range(8)], axis=1)
        split(rows, pl.multiple_of(512 + slot * 32, 32))
        return carry

    def transform(n, carry):
        at = pl.multiple_of(n * 256, 256)
        high = xh[pl.ds(at, 256), :]
        low = xlo[pl.ds(at, 256), :]
        spec = dot_nt(th[...], high) + dot_nt(th[...], low) + dot_nt(tl[...], high)
        mask = lane_bit((F, 128), 5)
        for t in range(2):
            re = spec[:F, t * 128:(t + 1) * 128]
            im = spec[F:, t * 128:(t + 1) * 128]
            row = (n // 2) * 8 + (n % 2) * 4 + 2 * t
            u[pl.ds(row, F, stride=16), :] = jnp.where(mask, re, pltpu.roll(im, 32, 1))
            u[pl.ds(row + 1, F, stride=16), :] = jnp.where(mask, pltpu.roll(re, 96, 1), im)
        return carry

    lax.fori_loop(0, 8, split_a, 0)
    lax.fori_loop(0, 2, transform, 0)
    for item in rec_loads:
        item.wait()
    lax.fori_loop(0, 16, split_b, 0)
    lax.fori_loop(2, 4, transform, 0)

    pl.semaphore_wait(barrier, ns + nm - 1)

    def s1(k, to, frm):
        return pltpu.make_async_remote_copy(
            src_ref=s_buf.at[to], dst_ref=r1.at[frm], send_sem=s1_send.at[k], recv_sem=s1_recv.at[k],
            device_id={"src": to, "xl": j}, device_id_type=MESH)

    def s1_go(k, carry):
        to = (me + k) % ns
        s_buf[to] = u[pl.ds(pl.multiple_of(to * 128, 128), 128), :].astype(BF)
        s1(k, to, me).start()
        return carry

    lax.fori_loop(1, ns, s1_go, 0)
    r1[me] = u[pl.ds(pl.multiple_of(me * 128, 128), 128), :].astype(BF)

    def s1_wait(k, carry):
        s1(k, (me + k) % ns, (me + ns - k) % ns).wait()
        return carry

    lax.fori_loop(1, ns, s1_wait, 0)

    def s2(k, to, frm):
        return pltpu.make_async_remote_copy(
            src_ref=r1.at[:, pl.ds(pl.multiple_of(to * 16, 16), 16), :], dst_ref=r2.at[frm],
            send_sem=s2_send.at[k], recv_sem=s2_recv.at[k],
            device_id={"src": me, "xl": to * Q + q}, device_id_type=MESH)

    def s2_go(k, carry):
        s2(k, (my_y + k) % ny, my_y).start()
        return carry

    def s2_wait(k, carry):
        s2(k, (my_y + k) % ny, (my_y + ny - k) % ny).wait()
        return carry

    lax.fori_loop(1, ny, s2_go, 0)
    own = pltpu.make_async_copy(r1.at[:, pl.ds(pl.multiple_of(my_y * 16, 16), 16), :], r2.at[my_y], loc_sem)
    own.start()
    own.wait()
    lax.fori_loop(1, ny, s2_wait, 0)

    def arrange(i2, carry):
        top = lane_bit((16, 128), 6)
        real = lane_bit((16, 128), 5)
        for p in range(4):
            w = []
            for e in range(2):
                u0 = r2[2 * p, 2 * i2 + e].astype(F32)
                u1 = r2[2 * p + 1, 2 * i2 + e].astype(F32)
                w.append((jnp.where(top, u0, pltpu.roll(u1, 64, 1)), jnp.where(top, pltpu.roll(u0, 64, 1), u1)))
                rows = jnp.concatenate([w[e][0][:8], w[e][1][:8]], axis=0)
                acat[pl.ds(pl.multiple_of(i2 * 32 + e * 16, 16), 16), p * 128:(p + 1) * 128] = rows.astype(BF)
            for ra in range(2):
                rows = jnp.concatenate([w[0][ra][8:], w[1][ra][8:]], axis=0)
                at = pl.multiple_of(i2 * 16, 16)
                bb[ra, pl.ds(at, 16), p * 128:(p + 1) * 128] = jnp.where(real, rows, -rows).astype(BF)
                swapped = jnp.where(real, pltpu.roll(rows, 96, 1), pltpu.roll(rows, 32, 1))
                bb[ra, pl.ds(128 + at, 16), p * 128:(p + 1) * 128] = swapped.astype(BF)
        return carry

    lax.fori_loop(0, ns // 2, arrange, 0)

    prod = dot_nt(acat[...], bb[1 - c])
    psend[0] = prod[:, :128]
    psend[1] = prod[:, 128:]
    pair = pltpu.make_async_remote_copy(
        src_ref=psend, dst_ref=precv, send_sem=p_sem.at[0], recv_sem=p_sem.at[1],
        device_id={"src": me, "xl": m * 2 + 1 - c}, device_id_type=MESH)
    pair.start()
    prod = dot_nt(acat[...], bb[c])
    cown[0] = prod[:, :128]
    cown[1] = prod[:, 128:]
    pair.wait()

    theirs = pl.ds(pl.multiple_of((1 - hi) * 128, 128), 128)
    mine = pl.ds(pl.multiple_of(hi * 128, 128), 128)
    for z in range(2):
        xsend[z] = (cown[z, theirs, :] + precv[z, theirs, :]).astype(BF)
    cross = pltpu.make_async_remote_copy(
        src_ref=xsend, dst_ref=xrecv, send_sem=x_sem.at[0], recv_sem=x_sem.at[1],
        device_id={"src": me, "xl": (my_y * 2 + 1 - hi) * 2 + c}, device_id_type=MESH)
    cross.start()
    for z in range(2):
        ck[pl.ds(z * 128, 128), :] = cown[z, mine, :] + precv[z, mine, :]
    cross.wait()
    for z in range(2):
        ck[pl.ds(z * 128, 128), :] += xrecv[z].astype(F32)

    halves = []
    for z in range(2):
        v = jnp.concatenate([ck[pl.ds(z * 128 + sp, 8, stride=16), :] for sp in range(16)], axis=0)
        for b in range(4):
            step = 8 << b
            v = v.reshape(8 >> b, 2, 8 << b, 128)
            low, high = v[:, 0].reshape(64, 128), v[:, 1].reshape(64, 128)
            keep = lane_bit((64, 128), b + 3)
            new_low = jnp.where(keep, low, pltpu.roll(high, step, 1))
            new_high = jnp.where(keep, pltpu.roll(low, 128 - step, 1), high)
            parts = (8 >> b, 1, 8 << b, 128)
            v = jnp.concatenate([new_low.reshape(parts), new_high.reshape(parts)], axis=1).reshape(128, 128)
        halves.append(v.reshape(16, 8, 128))
    d_buf[...] = jnp.concatenate(halves, axis=1).astype(BF)

    def c1(k, to, frm):
        return pltpu.make_async_remote_copy(
            src_ref=d_buf.at[to], dst_ref=e_buf.at[frm], send_sem=c1_send.at[k], recv_sem=c1_recv.at[k],
            device_id={"src": me, "xl": to * 2 + c}, device_id_type=MESH)

    def c1_go(k, carry):
        c1(k, (m + k) % nm, m).start()
        return carry

    def c1_wait(k, carry):
        c1(k, (m + k) % nm, (m + nm - k) % nm).wait()
        return carry

    lax.fori_loop(1, nm, c1_go, 0)
    e_buf[m] = d_buf[m]
    lax.fori_loop(1, nm, c1_wait, 0)

    for half in range(2):
        for y in range(ny):
            tile = e_buf[2 * y + half].astype(F32)
            t_buf[pl.ds(half * 128 + y, 8, stride=16), :] = tile[:8]
            t_buf[pl.ds(half * 128 + 8 + y, 8, stride=16), :] = tile[8:]
    h_buf[...] = t_buf[...].reshape(16, 16, 128).astype(BF)

    def c2(k, to, frm):
        return pltpu.make_async_remote_copy(
            src_ref=h_buf.at[to], dst_ref=g_buf.at[frm], send_sem=c2_send.at[k], recv_sem=c2_recv.at[k],
            device_id={"src": to, "xl": j}, device_id_type=MESH)

    def c2_go(k, carry):
        c2(k, (me + k) % ns, me).start()
        return carry

    def c2_wait(k, carry):
        c2(k, (me + k) % ns, (me + ns - k) % ns).wait()
        return carry

    lax.fori_loop(1, ns, c2_go, 0)
    g_buf[me] = h_buf[me]
    lax.fori_loop(1, ns, c2_wait, 0)

    got = g_buf[...].astype(F32)
    for z in range(2):
        flat = got[:, z * 8:(z + 1) * 8, :].reshape(F, 128)
        turned = flat.T * scale
        for s in range(16):
            sp = (s >> 1 & 1) * 8 + (s >> 2) * 2 + (s & 1)
            out_ref[s, :, z * F:(z + 1) * F] = turned[sp * 8:(sp + 1) * 8]


def per_device(ns, nx, src_traces, rec_traces):
    ny = nx // Q
    s, x, samples = src_traces.shape
    r = rec_traces.shape[1]
    scale = 1.0 / math.sqrt(x * nx)
    high, low = fourier_parts(samples)
    rows = s * x
    rec = rec_traces.reshape(rows, samples)
    out_shape = jax.ShapeDtypeStruct((s, r * ns // nx, 2 * F), F32)
    dma = pltpu.SemaphoreType.DMA
    nm = 2 * ny
    any_spec = pl.BlockSpec(memory_space=pl.ANY)
    return pl.pallas_call(
        functools.partial(kernel, ns, ny, scale),
        out_shape=out_shape,
        in_specs=[any_spec] * 4,
        out_specs=pl.BlockSpec(memory_space=pltpu.VMEM),
        scratch_shapes=[
            pltpu.VMEM((rows, samples), F32),
            pltpu.VMEM((8, rows, 128), F32),
            pltpu.VMEM((2 * F, samples), BF),
            pltpu.VMEM((2 * F, samples), BF),
            pltpu.VMEM((2 * rows, samples), BF),
            pltpu.VMEM((2 * rows, samples), BF),
            pltpu.VMEM((F * 16, 128), F32),
            pltpu.VMEM((ns, 128, 128), BF),
            pltpu.VMEM((ns, 128, 128), BF),
            pltpu.VMEM((ny, ns, 16, 128), BF),
            pltpu.VMEM((256, 512), BF),
            pltpu.VMEM((2, 256, 512), BF),
            pltpu.VMEM((2, 256, 128), F32),
            pltpu.VMEM((2, 256, 128), F32),
            pltpu.VMEM((2, 256, 128), F32),
            pltpu.VMEM((2, 128, 128), BF),
            pltpu.VMEM((2, 128, 128), BF),
            pltpu.VMEM((256, 128), F32),
            pltpu.VMEM((16, 16, 128), BF),
            pltpu.VMEM((16, 16, 128), BF),
            pltpu.VMEM((256, 128), F32),
            pltpu.VMEM((16, 16, 128), BF),
            pltpu.VMEM((16, 16, 128), BF),
            dma((11,)), dma((ns,)), dma((ns,)), dma((ny,)), dma((ny,)), dma, dma((2,)), dma((2,)),
            dma((nm,)), dma((nm,)), dma((ns,)), dma((ns,)),
        ],
        compiler_params=pltpu.CompilerParams(
            collective_id=0, has_side_effects=True, vmem_limit_bytes=56 << 20),
    )(src_traces.reshape(rows, samples), rec, jnp.asarray(high), jnp.asarray(low))


def solution(mesh):
    body = functools.partial(per_device, mesh.shape["src"], mesh.shape["xl"])
    return jax.shard_map(
        body,
        mesh=mesh,
        in_specs=(P("src", "xl", None), P("xl", "src", None)),
        out_specs=P("src", "xl", None),
        check_vma=False,
    )
```

```python
import functools
import math

import jax
import jax.numpy as jnp
import numpy as np
from jax import lax
from jax.experimental import pallas as pl
from jax.experimental.pallas import tpu as pltpu
from jax.sharding import PartitionSpec as P

F = 128
FBASE = 4
Q = 4
BF = jnp.bfloat16
F32 = jnp.float32
MESH = pl.DeviceIdType.MESH
NT = (((1,), (1,)), ((), ()))


def fourier_parts(samples):
    times = np.arange(samples, dtype=np.int64)
    bins = FBASE + np.arange(F, dtype=np.int64)
    angles = (bins[:, None] * times[None, :] % samples) * (2.0 * math.pi / samples)
    table = np.concatenate([np.cos(angles), -np.sin(angles)], axis=0) / math.sqrt(samples)
    table = table.astype(np.float32)
    high = table.astype(jnp.bfloat16)
    low = (table - high.astype(np.float32)).astype(jnp.bfloat16)
    return high, low


def dot_nt(a, b):
    return lax.dot_general(a, b, NT, preferred_element_type=F32)


def lane_bit(shape, bit):
    lanes = lax.broadcasted_iota(jnp.int32, shape, len(shape) - 1)
    return ((lanes >> bit) & 1) == 0


def kernel(ns, ny, scale, src_ref, rec_ref, thi_ref, tlo_ref, out_ref,
           xa, xb, th, tl, xh, xlo, u, s_buf, r2, acat, bb,
           psend, precv, cown, xsend, xrecv, ck, d_buf, e_buf, t_buf, h_buf, g_buf,
           in_sem, s_send, s_recv, p_sem, x_sem,
           c1_send, c1_recv, c2_send, c2_recv):
    me = lax.axis_index("src")
    j = lax.axis_index("xl")
    my_y = j // Q
    q = j % Q
    m = j // 2
    c = j % 2
    hi = m % 2
    nm = 2 * ny

    def load(a, b, k):
        return pltpu.make_async_copy(a, b, in_sem.at[k])

    loads = [load(thi_ref, th, 0), load(tlo_ref, tl, 1), load(src_ref, xa, 2)]
    rec_loads = [load(rec_ref.at[:, pl.ds(t * 128, 128)], xb.at[t], 3 + t) for t in range(8)]
    for item in loads + rec_loads:
        item.start()

    barrier = pltpu.get_barrier_semaphore()

    def greet(k, carry):
        to = {"src": (me + k // ny) % ns, "xl": (my_y + k) % ny * Q + q}
        pl.semaphore_signal(barrier, inc=1, device_id=to, device_id_type=MESH)
        return carry

    def greet_x(k, carry):
        pl.semaphore_signal(barrier, inc=1, device_id={"src": me, "xl": k * Q + (1 - hi) * 2 + c}, device_id_type=MESH)
        return carry

    lax.fori_loop(1, ns * ny, greet, 0)
    lax.fori_loop(0, ny, greet_x, 0)
    pl.semaphore_signal(barrier, inc=1, device_id={"src": me, "xl": m * 2 + 1 - c}, device_id_type=MESH)

    for item in loads:
        item.wait()

    def split(rows, start):
        high = rows.astype(BF)
        xh[pl.ds(start, rows.shape[0]), :] = high
        xlo[pl.ds(start, rows.shape[0]), :] = (rows - high.astype(F32)).astype(BF)

    def split_a(k, carry):
        at = pl.multiple_of(k * 64, 64)
        split(xa[pl.ds(at, 64), :], at)
        return carry

    def split_b(r, carry):
        slot = (r % 8) // 2 * 4 + (r // 8) * 2 + r % 2
        rows = jnp.concatenate([xb[t, pl.ds(r, 32, stride=16), :] for t in range(8)], axis=1)
        split(rows, pl.multiple_of(512 + slot * 32, 32))
        return carry

    def transform(n, carry):
        at = pl.multiple_of(n * 256, 256)
        high = xh[pl.ds(at, 256), :]
        low = xlo[pl.ds(at, 256), :]
        spec = dot_nt(th[...], high) + dot_nt(th[...], low) + dot_nt(tl[...], high)
        mask = lane_bit((F, 128), 5)
        for t in range(2):
            re = spec[:F, t * 128:(t + 1) * 128]
            im = spec[F:, t * 128:(t + 1) * 128]
            row = (n // 2) * 8 + (n % 2) * 4 + 2 * t
            u[pl.ds(row, F, stride=16), :] = jnp.where(mask, re, pltpu.roll(im, 32, 1))
            u[pl.ds(row + 1, F, stride=16), :] = jnp.where(mask, pltpu.roll(re, 96, 1), im)
        return carry

    lax.fori_loop(0, 8, split_a, 0)
    lax.fori_loop(0, 2, transform, 0)
    for item in rec_loads:
        item.wait()
    lax.fori_loop(0, 16, split_b, 0)
    lax.fori_loop(2, 4, transform, 0)

    pl.semaphore_wait(barrier, ns * ny + ny)

    def convert(k, carry):
        to = (me + k) % ns
        s_buf[to] = u[pl.ds(pl.multiple_of(to * 128, 128), 128), :].astype(BF).reshape(8, 16, 128)

        def go(y, inner):
            to_y = (my_y + y) % ny
            pltpu.make_async_remote_copy(
                src_ref=s_buf.at[to, to_y], dst_ref=r2.at[me, my_y], send_sem=s_send, recv_sem=s_recv.at[me],
                device_id={"src": to, "xl": to_y * Q + q}, device_id_type=MESH).start()
            return inner

        lax.fori_loop(lax.select(k == 0, 1, 0), ny, go, 0)
        return carry

    lax.fori_loop(0, ns, convert, 0)
    pltpu.make_async_copy(s_buf.at[me, my_y], r2.at[me, my_y], s_recv.at[me]).start()

    def arrange(i2, carry):
        top = lane_bit((16, 128), 6)
        real = lane_bit((16, 128), 5)
        for e in range(2):
            pltpu.make_async_copy(r2.at[2 * i2 + e], r2.at[2 * i2 + e], s_recv.at[2 * i2 + e]).wait()
        for p in range(4):
            w = []
            for e in range(2):
                u0 = r2[2 * i2 + e, 2 * p].astype(F32)
                u1 = r2[2 * i2 + e, 2 * p + 1].astype(F32)
                w.append((jnp.where(top, u0, pltpu.roll(u1, 64, 1)), jnp.where(top, pltpu.roll(u0, 64, 1), u1)))
                rows = jnp.concatenate([w[e][0][:8], w[e][1][:8]], axis=0)
                acat[pl.ds(pl.multiple_of(i2 * 32 + e * 16, 16), 16), p * 128:(p + 1) * 128] = rows.astype(BF)
            for ra in range(2):
                rows = jnp.concatenate([w[0][ra][8:], w[1][ra][8:]], axis=0)
                at = pl.multiple_of(i2 * 16, 16)
                bb[ra, pl.ds(at, 16), p * 128:(p + 1) * 128] = jnp.where(real, rows, -rows).astype(BF)
                swapped = jnp.where(real, pltpu.roll(rows, 96, 1), pltpu.roll(rows, 32, 1))
                bb[ra, pl.ds(128 + at, 16), p * 128:(p + 1) * 128] = swapped.astype(BF)
        return carry

    lax.fori_loop(0, ns // 2, arrange, 0)
    for part in (s_buf.at[pl.ds(0, ns - 1)], s_buf.at[0, pl.ds(0, ny - 1)]):
        pltpu.make_async_copy(part, part, s_send).wait()

    prod = dot_nt(acat[...], bb[1 - c])
    psend[0] = prod[:, :128]
    psend[1] = prod[:, 128:]
    pair = pltpu.make_async_remote_copy(
        src_ref=psend, dst_ref=precv, send_sem=p_sem.at[0], recv_sem=p_sem.at[1],
        device_id={"src": me, "xl": m * 2 + 1 - c}, device_id_type=MESH)
    pair.start()
    prod = dot_nt(acat[...], bb[c])
    cown[0] = prod[:, :128]
    cown[1] = prod[:, 128:]
    pair.wait()

    theirs = pl.ds(pl.multiple_of((1 - hi) * 128, 128), 128)
    mine = pl.ds(pl.multiple_of(hi * 128, 128), 128)
    for z in range(2):
        xsend[z] = (cown[z, theirs, :] + precv[z, theirs, :]).astype(BF)
    cross = pltpu.make_async_remote_copy(
        src_ref=xsend, dst_ref=xrecv, send_sem=x_sem.at[0], recv_sem=x_sem.at[1],
        device_id={"src": me, "xl": (my_y * 2 + 1 - hi) * 2 + c}, device_id_type=MESH)
    cross.start()
    for z in range(2):
        ck[pl.ds(z * 128, 128), :] = cown[z, mine, :] + precv[z, mine, :]
    cross.wait()
    for z in range(2):
        ck[pl.ds(z * 128, 128), :] += xrecv[z].astype(F32)

    halves = []
    for z in range(2):
        v = jnp.concatenate([ck[pl.ds(z * 128 + sp, 8, stride=16), :] for sp in range(16)], axis=0)
        for b in range(4):
            step = 8 << b
            v = v.reshape(8 >> b, 2, 8 << b, 128)
            low, high = v[:, 0].reshape(64, 128), v[:, 1].reshape(64, 128)
            keep = lane_bit((64, 128), b + 3)
            new_low = jnp.where(keep, low, pltpu.roll(high, step, 1))
            new_high = jnp.where(keep, pltpu.roll(low, 128 - step, 1), high)
            parts = (8 >> b, 1, 8 << b, 128)
            v = jnp.concatenate([new_low.reshape(parts), new_high.reshape(parts)], axis=1).reshape(128, 128)
        halves.append(v.reshape(16, 8, 128))
    d_buf[...] = jnp.concatenate(halves, axis=1).astype(BF)

    def c1(k, to, frm):
        return pltpu.make_async_remote_copy(
            src_ref=d_buf.at[to], dst_ref=e_buf.at[frm], send_sem=c1_send.at[k], recv_sem=c1_recv.at[k],
            device_id={"src": me, "xl": to * 2 + c}, device_id_type=MESH)

    def c1_go(k, carry):
        c1(k, (m + k) % nm, m).start()
        return carry

    def c1_wait(k, carry):
        c1(k, (m + k) % nm, (m + nm - k) % nm).wait()
        return carry

    lax.fori_loop(1, nm, c1_go, 0)
    e_buf[m] = d_buf[m]
    lax.fori_loop(1, nm, c1_wait, 0)

    for half in range(2):
        for y in range(ny):
            tile = e_buf[2 * y + half].astype(F32)
            t_buf[pl.ds(half * 128 + y, 8, stride=16), :] = tile[:8]
            t_buf[pl.ds(half * 128 + 8 + y, 8, stride=16), :] = tile[8:]
    h_buf[...] = t_buf[...].reshape(16, 16, 128).astype(BF)

    def c2(k, to, frm):
        return pltpu.make_async_remote_copy(
            src_ref=h_buf.at[to], dst_ref=g_buf.at[frm], send_sem=c2_send.at[k], recv_sem=c2_recv.at[k],
            device_id={"src": to, "xl": j}, device_id_type=MESH)

    def c2_go(k, carry):
        c2(k, (me + k) % ns, me).start()
        return carry

    def c2_wait(k, carry):
        c2(k, (me + k) % ns, (me + ns - k) % ns).wait()
        return carry

    lax.fori_loop(1, ns, c2_go, 0)
    g_buf[me] = h_buf[me]
    lax.fori_loop(1, ns, c2_wait, 0)

    got = g_buf[...].astype(F32)
    for z in range(2):
        flat = got[:, z * 8:(z + 1) * 8, :].reshape(F, 128)
        turned = flat.T * scale
        for s in range(16):
            sp = (s >> 1 & 1) * 8 + (s >> 2) * 2 + (s & 1)
            out_ref[s, :, z * F:(z + 1) * F] = turned[sp * 8:(sp + 1) * 8]


def per_device(ns, nx, src_traces, rec_traces):
    ny = nx // Q
    s, x, samples = src_traces.shape
    r = rec_traces.shape[1]
    scale = 1.0 / math.sqrt(x * nx)
    high, low = fourier_parts(samples)
    rows = s * x
    rec = rec_traces.reshape(rows, samples)
    out_shape = jax.ShapeDtypeStruct((s, r * ns // nx, 2 * F), F32)
    dma = pltpu.SemaphoreType.DMA
    nm = 2 * ny
    any_spec = pl.BlockSpec(memory_space=pl.ANY)
    return pl.pallas_call(
        functools.partial(kernel, ns, ny, scale),
        out_shape=out_shape,
        in_specs=[any_spec] * 4,
        out_specs=pl.BlockSpec(memory_space=pltpu.VMEM),
        scratch_shapes=[
            pltpu.VMEM((rows, samples), F32),
            pltpu.VMEM((8, rows, 128), F32),
            pltpu.VMEM((2 * F, samples), BF),
            pltpu.VMEM((2 * F, samples), BF),
            pltpu.VMEM((2 * rows, samples), BF),
            pltpu.VMEM((2 * rows, samples), BF),
            pltpu.VMEM((F * 16, 128), F32),
            pltpu.VMEM((ns, ny, 16, 128), BF),
            pltpu.VMEM((ns, ny, 16, 128), BF),
            pltpu.VMEM((256, 512), BF),
            pltpu.VMEM((2, 256, 512), BF),
            pltpu.VMEM((2, 256, 128), F32),
            pltpu.VMEM((2, 256, 128), F32),
            pltpu.VMEM((2, 256, 128), F32),
            pltpu.VMEM((2, 128, 128), BF),
            pltpu.VMEM((2, 128, 128), BF),
            pltpu.VMEM((256, 128), F32),
            pltpu.VMEM((16, 16, 128), BF),
            pltpu.VMEM((16, 16, 128), BF),
            pltpu.VMEM((256, 128), F32),
            pltpu.VMEM((16, 16, 128), BF),
            pltpu.VMEM((16, 16, 128), BF),
            dma((11,)), dma, dma((ns,)), dma((2,)), dma((2,)),
            dma((nm,)), dma((nm,)), dma((ns,)), dma((ns,)),
        ],
        compiler_params=pltpu.CompilerParams(
            collective_id=0, has_side_effects=True, vmem_limit_bytes=56 << 20),
    )(src_traces.reshape(rows, samples), rec, jnp.asarray(high), jnp.asarray(low))


def solution(mesh):
    body = functools.partial(per_device, mesh.shape["src"], mesh.shape["xl"])
    return jax.shard_map(
        body,
        mesh=mesh,
        in_specs=(P("src", "xl", None), P("xl", "src", None)),
        out_specs=P("src", "xl", None),
        check_vma=False,
    )
```

```python
import functools
import math

import jax
import jax.numpy as jnp
import numpy as np
from jax import lax
from jax.experimental import pallas as pl
from jax.experimental.pallas import tpu as pltpu
from jax.sharding import PartitionSpec as P

F = 128
FBASE = 4
Q = 4
BF = jnp.bfloat16
F32 = jnp.float32
MESH = pl.DeviceIdType.MESH
NT = (((1,), (1,)), ((), ()))


def fourier_parts(samples):
    times = np.arange(samples, dtype=np.int64)
    bins = FBASE + np.arange(F, dtype=np.int64)
    angles = (bins[:, None] * times[None, :] % samples) * (2.0 * math.pi / samples)
    table = np.concatenate([np.cos(angles), -np.sin(angles)], axis=0) / math.sqrt(samples)
    table = table.astype(np.float32)
    high = table.astype(jnp.bfloat16)
    low = (table - high.astype(np.float32)).astype(jnp.bfloat16)
    return high, low


def dot_nt(a, b):
    return lax.dot_general(a, b, NT, preferred_element_type=F32)


def lane_bit(shape, bit):
    lanes = lax.broadcasted_iota(jnp.int32, shape, len(shape) - 1)
    return ((lanes >> bit) & 1) == 0


def kernel(ns, ny, scale, src_ref, rec_ref, thi_ref, tlo_ref, out_ref,
           xa, xb, th, tl, xh, xlo, u, s_buf, r2, acat, bb,
           psend, precv, cown, xsend, xrecv, ck, d_buf, e_buf, t_buf, h_buf, g_buf,
           in_sem, s_send, s_recv, p_sem, x_sem,
           c1_send, c1_recv, c2_send, c2_recv, ready):
    me = lax.axis_index("src")
    j = lax.axis_index("xl")
    my_y = j // Q
    q = j % Q
    m = j // 2
    c = j % 2
    hi = m % 2
    nm = 2 * ny

    def load(a, b, k):
        return pltpu.make_async_copy(a, b, in_sem.at[k])

    loads = [load(thi_ref, th, 0), load(tlo_ref, tl, 1), load(src_ref, xa, 2)]
    rec_loads = [load(rec_ref.at[:, pl.ds(t * 128, 128)], xb.at[t], 3 + t) for t in range(8)]
    for item in loads + rec_loads:
        item.start()

    barrier = pltpu.get_barrier_semaphore()

    def greet_src(k, carry):
        pl.semaphore_signal(barrier, inc=1, device_id={"src": (me + k) % ns, "xl": j}, device_id_type=MESH)
        return carry

    def greet_y(k, carry):
        pl.semaphore_signal(barrier, inc=1, device_id={"src": me, "xl": (my_y + k) % ny * Q + q}, device_id_type=MESH)
        return carry

    def row_ready(k, carry):
        pl.semaphore_signal(ready, inc=1, device_id={"src": (me + k) % ns, "xl": j}, device_id_type=MESH)
        return carry

    def greet_x(k, carry):
        pl.semaphore_signal(barrier, inc=1, device_id={"src": me, "xl": k * Q + (1 - hi) * 2 + c}, device_id_type=MESH)
        return carry

    lax.fori_loop(1, ns, greet_src, 0)
    lax.fori_loop(1, ny, greet_y, 0)
    lax.fori_loop(0, ny, greet_x, 0)
    pl.semaphore_signal(barrier, inc=1, device_id={"src": me, "xl": m * 2 + 1 - c}, device_id_type=MESH)

    for item in loads:
        item.wait()

    def split(rows, start):
        high = rows.astype(BF)
        xh[pl.ds(start, rows.shape[0]), :] = high
        xlo[pl.ds(start, rows.shape[0]), :] = (rows - high.astype(F32)).astype(BF)

    def split_a(k, carry):
        at = pl.multiple_of(k * 64, 64)
        split(xa[pl.ds(at, 64), :], at)
        return carry

    def split_b(r, carry):
        slot = (r % 8) // 2 * 4 + (r // 8) * 2 + r % 2
        rows = jnp.concatenate([xb[t, pl.ds(r, 32, stride=16), :] for t in range(8)], axis=1)
        split(rows, pl.multiple_of(512 + slot * 32, 32))
        return carry

    def transform(n, carry):
        at = pl.multiple_of(n * 256, 256)
        high = xh[pl.ds(at, 256), :]
        low = xlo[pl.ds(at, 256), :]
        spec = dot_nt(th[...], high) + dot_nt(th[...], low) + dot_nt(tl[...], high)
        mask = lane_bit((F, 128), 5)
        for t in range(2):
            re = spec[:F, t * 128:(t + 1) * 128]
            im = spec[F:, t * 128:(t + 1) * 128]
            row = (n // 2) * 8 + (n % 2) * 4 + 2 * t
            u[pl.ds(row, F, stride=16), :] = jnp.where(mask, re, pltpu.roll(im, 32, 1))
            u[pl.ds(row + 1, F, stride=16), :] = jnp.where(mask, pltpu.roll(re, 96, 1), im)
        return carry

    lax.fori_loop(0, 8, split_a, 0)
    lax.fori_loop(0, 2, transform, 0)
    for item in rec_loads:
        item.wait()
    lax.fori_loop(0, 16, split_b, 0)
    lax.fori_loop(2, 4, transform, 0)

    pl.semaphore_wait(barrier, ns + 2 * ny - 1)
    lax.fori_loop(1, ns, row_ready, 0)
    for k in range(ns):
        s_buf[k] = u[k * 128:(k + 1) * 128, :].astype(BF).reshape(8, 16, 128)
    pl.semaphore_wait(ready, ns - 1)

    def go(k, carry):
        order = k * 37 % (ns * ny)
        to = (me + order // ny) % ns
        to_y = (my_y + order) % ny
        pltpu.make_async_remote_copy(
            src_ref=s_buf.at[to, to_y], dst_ref=r2.at[me, my_y], send_sem=s_send, recv_sem=s_recv.at[me],
            device_id={"src": to, "xl": to_y * Q + q}, device_id_type=MESH).start()
        return carry

    lax.fori_loop(1, ns * ny, go, 0)
    pltpu.make_async_copy(s_buf.at[me, my_y], r2.at[me, my_y], s_recv.at[me]).start()

    def arrange(i2, carry):
        top = lane_bit((16, 128), 6)
        real = lane_bit((16, 128), 5)
        for e in range(2):
            pltpu.make_async_copy(r2.at[2 * i2 + e], r2.at[2 * i2 + e], s_recv.at[2 * i2 + e]).wait()
        for p in range(4):
            w = []
            for e in range(2):
                u0 = r2[2 * i2 + e, 2 * p].astype(F32)
                u1 = r2[2 * i2 + e, 2 * p + 1].astype(F32)
                w.append((jnp.where(top, u0, pltpu.roll(u1, 64, 1)), jnp.where(top, pltpu.roll(u0, 64, 1), u1)))
                rows = jnp.concatenate([w[e][0][:8], w[e][1][:8]], axis=0)
                acat[pl.ds(pl.multiple_of(i2 * 32 + e * 16, 16), 16), p * 128:(p + 1) * 128] = rows.astype(BF)
            for ra in range(2):
                rows = jnp.concatenate([w[0][ra][8:], w[1][ra][8:]], axis=0)
                at = pl.multiple_of(i2 * 16, 16)
                bb[ra, pl.ds(at, 16), p * 128:(p + 1) * 128] = jnp.where(real, rows, -rows).astype(BF)
                swapped = jnp.where(real, pltpu.roll(rows, 96, 1), pltpu.roll(rows, 32, 1))
                bb[ra, pl.ds(128 + at, 16), p * 128:(p + 1) * 128] = swapped.astype(BF)
        return carry

    lax.fori_loop(0, ns // 2, arrange, 0)
    for part in (s_buf.at[pl.ds(0, ns - 1)], s_buf.at[0, pl.ds(0, ny - 1)]):
        pltpu.make_async_copy(part, part, s_send).wait()

    prod = dot_nt(acat[...], bb[1 - c])
    psend[0] = prod[:, :128]
    psend[1] = prod[:, 128:]
    pair = pltpu.make_async_remote_copy(
        src_ref=psend, dst_ref=precv, send_sem=p_sem.at[0], recv_sem=p_sem.at[1],
        device_id={"src": me, "xl": m * 2 + 1 - c}, device_id_type=MESH)
    pair.start()
    prod = dot_nt(acat[...], bb[c])
    cown[0] = prod[:, :128]
    cown[1] = prod[:, 128:]
    pair.wait()

    theirs = pl.ds(pl.multiple_of((1 - hi) * 128, 128), 128)
    mine = pl.ds(pl.multiple_of(hi * 128, 128), 128)
    for z in range(2):
        xsend[z] = (cown[z, theirs, :] + precv[z, theirs, :]).astype(BF)
    cross = pltpu.make_async_remote_copy(
        src_ref=xsend, dst_ref=xrecv, send_sem=x_sem.at[0], recv_sem=x_sem.at[1],
        device_id={"src": me, "xl": (my_y * 2 + 1 - hi) * 2 + c}, device_id_type=MESH)
    cross.start()
    for z in range(2):
        ck[pl.ds(z * 128, 128), :] = cown[z, mine, :] + precv[z, mine, :]
    cross.wait()
    for z in range(2):
        ck[pl.ds(z * 128, 128), :] += xrecv[z].astype(F32)

    halves = []
    for z in range(2):
        v = jnp.concatenate([ck[pl.ds(z * 128 + sp, 8, stride=16), :] for sp in range(16)], axis=0)
        for b in range(4):
            step = 8 << b
            v = v.reshape(8 >> b, 2, 8 << b, 128)
            low, high = v[:, 0].reshape(64, 128), v[:, 1].reshape(64, 128)
            keep = lane_bit((64, 128), b + 3)
            new_low = jnp.where(keep, low, pltpu.roll(high, step, 1))
            new_high = jnp.where(keep, pltpu.roll(low, 128 - step, 1), high)
            parts = (8 >> b, 1, 8 << b, 128)
            v = jnp.concatenate([new_low.reshape(parts), new_high.reshape(parts)], axis=1).reshape(128, 128)
        halves.append(v.reshape(16, 8, 128))
    d_buf[...] = jnp.concatenate(halves, axis=1).astype(BF)

    def c1(k, to, frm):
        return pltpu.make_async_remote_copy(
            src_ref=d_buf.at[to], dst_ref=e_buf.at[frm], send_sem=c1_send.at[k], recv_sem=c1_recv.at[k],
            device_id={"src": me, "xl": to * 2 + c}, device_id_type=MESH)

    def c1_go(k, carry):
        c1(k, (m + k) % nm, m).start()
        return carry

    def c1_wait(k, carry):
        c1(k, (m + k) % nm, (m + nm - k) % nm).wait()
        return carry

    lax.fori_loop(1, nm, c1_go, 0)
    e_buf[m] = d_buf[m]
    lax.fori_loop(1, nm, c1_wait, 0)

    for half in range(2):
        for y in range(ny):
            tile = e_buf[2 * y + half].astype(F32)
            t_buf[pl.ds(half * 128 + y, 8, stride=16), :] = tile[:8]
            t_buf[pl.ds(half * 128 + 8 + y, 8, stride=16), :] = tile[8:]
    h_buf[...] = t_buf[...].reshape(16, 16, 128).astype(BF)

    def c2(k, to, frm):
        return pltpu.make_async_remote_copy(
            src_ref=h_buf.at[to], dst_ref=g_buf.at[frm], send_sem=c2_send.at[k], recv_sem=c2_recv.at[k],
            device_id={"src": to, "xl": j}, device_id_type=MESH)

    def c2_go(k, carry):
        c2(k, (me + k) % ns, me).start()
        return carry

    def c2_wait(k, carry):
        c2(k, (me + k) % ns, (me + ns - k) % ns).wait()
        return carry

    lax.fori_loop(1, ns, c2_go, 0)
    g_buf[me] = h_buf[me]
    lax.fori_loop(1, ns, c2_wait, 0)

    got = g_buf[...].astype(F32)
    for z in range(2):
        flat = got[:, z * 8:(z + 1) * 8, :].reshape(F, 128)
        turned = flat.T * scale
        for s in range(16):
            sp = (s >> 1 & 1) * 8 + (s >> 2) * 2 + (s & 1)
            out_ref[s, :, z * F:(z + 1) * F] = turned[sp * 8:(sp + 1) * 8]


def per_device(ns, nx, src_traces, rec_traces):
    ny = nx // Q
    s, x, samples = src_traces.shape
    r = rec_traces.shape[1]
    scale = 1.0 / math.sqrt(x * nx)
    high, low = fourier_parts(samples)
    rows = s * x
    rec = rec_traces.reshape(rows, samples)
    out_shape = jax.ShapeDtypeStruct((s, r * ns // nx, 2 * F), F32)
    dma = pltpu.SemaphoreType.DMA
    nm = 2 * ny
    any_spec = pl.BlockSpec(memory_space=pl.ANY)
    return pl.pallas_call(
        functools.partial(kernel, ns, ny, scale),
        out_shape=out_shape,
        in_specs=[any_spec] * 4,
        out_specs=pl.BlockSpec(memory_space=pltpu.VMEM),
        scratch_shapes=[
            pltpu.VMEM((rows, samples), F32),
            pltpu.VMEM((8, rows, 128), F32),
            pltpu.VMEM((2 * F, samples), BF),
            pltpu.VMEM((2 * F, samples), BF),
            pltpu.VMEM((2 * rows, samples), BF),
            pltpu.VMEM((2 * rows, samples), BF),
            pltpu.VMEM((F * 16, 128), F32),
            pltpu.VMEM((ns, ny, 16, 128), BF),
            pltpu.VMEM((ns, ny, 16, 128), BF),
            pltpu.VMEM((256, 512), BF),
            pltpu.VMEM((2, 256, 512), BF),
            pltpu.VMEM((2, 256, 128), F32),
            pltpu.VMEM((2, 256, 128), F32),
            pltpu.VMEM((2, 256, 128), F32),
            pltpu.VMEM((2, 128, 128), BF),
            pltpu.VMEM((2, 128, 128), BF),
            pltpu.VMEM((256, 128), F32),
            pltpu.VMEM((16, 16, 128), BF),
            pltpu.VMEM((16, 16, 128), BF),
            pltpu.VMEM((256, 128), F32),
            pltpu.VMEM((16, 16, 128), BF),
            pltpu.VMEM((16, 16, 128), BF),
            dma((11,)), dma, dma((ns,)), dma((2,)), dma((2,)),
            dma((nm,)), dma((nm,)), dma((ns,)), dma((ns,)), pltpu.SemaphoreType.REGULAR,
        ],
        compiler_params=pltpu.CompilerParams(
            collective_id=0, has_side_effects=True, vmem_limit_bytes=56 << 20),
    )(src_traces.reshape(rows, samples), rec, jnp.asarray(high), jnp.asarray(low))


def solution(mesh):
    body = functools.partial(per_device, mesh.shape["src"], mesh.shape["xl"])
    return jax.shard_map(
        body,
        mesh=mesh,
        in_specs=(P("src", "xl", None), P("xl", "src", None)),
        out_specs=P("src", "xl", None),
        check_vma=False,
    )
```

```python
import functools
import math

import jax
import jax.numpy as jnp
import numpy as np
from jax import lax
from jax.experimental import pallas as pl
from jax.experimental.pallas import tpu as pltpu
from jax.sharding import PartitionSpec as P

F = 128
FBASE = 4
Q = 4
BF = jnp.bfloat16
F32 = jnp.float32
MESH = pl.DeviceIdType.MESH
NT = (((1,), (1,)), ((), ()))


def fourier_parts(samples):
    times = np.arange(samples, dtype=np.int64)
    bins = FBASE + np.arange(F, dtype=np.int64)
    angles = (bins[:, None] * times[None, :] % samples) * (2.0 * math.pi / samples)
    table = np.concatenate([np.cos(angles), -np.sin(angles)], axis=0) / math.sqrt(samples)
    table = table.astype(np.float32)
    high = table.astype(jnp.bfloat16)
    low = (table - high.astype(np.float32)).astype(jnp.bfloat16)
    return high, low


def dot_nt(a, b):
    return lax.dot_general(a, b, NT, preferred_element_type=F32)


def lane_bit(shape, bit):
    lanes = lax.broadcasted_iota(jnp.int32, shape, len(shape) - 1)
    return ((lanes >> bit) & 1) == 0


def kernel(ns, ny, scale, src_ref, rec_ref, thi_ref, tlo_ref, out_ref,
           xa, xb, th, tl, xh, xlo, u, s_buf, r2, acat, bb,
           psend, precv, cown, ck, d_buf, e_buf, t_buf, h_buf, g_buf,
           in_sem, s_send, s_recv, p_sem,
           c1_send, c1_recv, c2_send, c2_recv, ready):
    me = lax.axis_index("src")
    j = lax.axis_index("xl")
    my_y = j // Q
    q = j % Q
    m = j // 2
    c = j % 2
    hi = m % 2
    nm = 2 * ny

    def load(a, b, k):
        return pltpu.make_async_copy(a, b, in_sem.at[k])

    loads = [load(thi_ref, th, 0), load(tlo_ref, tl, 1), load(src_ref, xa, 2)]
    rec_loads = [load(rec_ref.at[:, pl.ds(t * 128, 128)], xb.at[t], 3 + t) for t in range(8)]
    for item in loads + rec_loads:
        item.start()

    barrier = pltpu.get_barrier_semaphore()

    def greet_src(k, carry):
        pl.semaphore_signal(barrier, inc=1, device_id={"src": (me + k) % ns, "xl": j}, device_id_type=MESH)
        return carry

    def greet_y(k, carry):
        pl.semaphore_signal(barrier, inc=1, device_id={"src": me, "xl": (my_y + k) % ny * Q + q}, device_id_type=MESH)
        return carry

    def row_ready(k, carry):
        pl.semaphore_signal(ready, inc=1, device_id={"src": (me + k) % ns, "xl": j}, device_id_type=MESH)
        return carry

    def greet_x(k, carry):
        pl.semaphore_signal(barrier, inc=1, device_id={"src": me, "xl": k * Q + (1 - hi) * 2 + c}, device_id_type=MESH)
        return carry

    lax.fori_loop(1, ns, greet_src, 0)
    lax.fori_loop(1, ny, greet_y, 0)
    lax.fori_loop(0, ny, greet_x, 0)
    pl.semaphore_signal(barrier, inc=1, device_id={"src": me, "xl": m * 2 + 1 - c}, device_id_type=MESH)

    for item in loads:
        item.wait()

    def split(rows, start):
        high = rows.astype(BF)
        xh[pl.ds(start, rows.shape[0]), :] = high
        xlo[pl.ds(start, rows.shape[0]), :] = (rows - high.astype(F32)).astype(BF)

    def split_a(k, carry):
        at = pl.multiple_of(k * 64, 64)
        split(xa[pl.ds(at, 64), :], at)
        return carry

    def split_b(r, carry):
        slot = (r % 8) // 2 * 4 + (r // 8) * 2 + r % 2
        rows = jnp.concatenate([xb[t, pl.ds(r, 32, stride=16), :] for t in range(8)], axis=1)
        split(rows, pl.multiple_of(512 + slot * 32, 32))
        return carry

    def transform(n, carry):
        at = pl.multiple_of(n * 256, 256)
        high = xh[pl.ds(at, 256), :]
        low = xlo[pl.ds(at, 256), :]
        spec = dot_nt(th[...], high) + dot_nt(th[...], low) + dot_nt(tl[...], high)
        mask = lane_bit((F, 128), 5)
        for t in range(2):
            re = spec[:F, t * 128:(t + 1) * 128]
            im = spec[F:, t * 128:(t + 1) * 128]
            row = (n // 2) * 8 + (n % 2) * 4 + 2 * t
            u[pl.ds(row, F, stride=16), :] = jnp.where(mask, re, pltpu.roll(im, 32, 1))
            u[pl.ds(row + 1, F, stride=16), :] = jnp.where(mask, pltpu.roll(re, 96, 1), im)
        return carry

    lax.fori_loop(0, 8, split_a, 0)
    pl.semaphore_wait(barrier, ns + 2 * ny - 1)
    lax.fori_loop(1, ns, row_ready, 0)
    lax.fori_loop(0, 2, transform, 0)
    for item in rec_loads:
        item.wait()
    lax.fori_loop(0, 16, split_b, 0)
    lax.fori_loop(2, 4, transform, 0)

    for k in range(ns):
        s_buf[k] = u[k * 128:(k + 1) * 128, :].astype(BF).reshape(8, 16, 128)

    def send(to, to_y):
        pltpu.make_async_remote_copy(
            src_ref=s_buf.at[to, to_y], dst_ref=r2.at[me, my_y], send_sem=s_send, recv_sem=s_recv.at[me],
            device_id={"src": to, "xl": to_y * Q + q}, device_id_type=MESH).start()

    def go_column(k, carry):
        send((me + k) % ns, my_y)
        return carry

    def go_row(k, carry):
        send(me, (my_y + k) % ny)
        return carry

    def go(k, carry):
        order = k * 37 % ((ns - 1) * (ny - 1))
        send((me + 1 + order // (ny - 1)) % ns, (my_y + 1 + order % (ny - 1)) % ny)
        return carry

    lax.fori_loop(1, ny, go_row, 0)
    lax.fori_loop(1, ns, go_column, 0)
    pl.semaphore_wait(ready, ns - 1)
    lax.fori_loop(0, (ns - 1) * (ny - 1), go, 0)
    pltpu.make_async_copy(s_buf.at[me, my_y], r2.at[me, my_y], s_recv.at[me]).start()

    def arrange(i2, carry):
        top = lane_bit((16, 128), 6)
        real = lane_bit((16, 128), 5)
        for e in range(2):
            pltpu.make_async_copy(r2.at[2 * i2 + e], r2.at[2 * i2 + e], s_recv.at[2 * i2 + e]).wait()
        for p in range(4):
            w = []
            for e in range(2):
                u0 = r2[2 * i2 + e, 2 * p].astype(F32)
                u1 = r2[2 * i2 + e, 2 * p + 1].astype(F32)
                w.append((jnp.where(top, u0, pltpu.roll(u1, 64, 1)), jnp.where(top, pltpu.roll(u0, 64, 1), u1)))
                rows = jnp.concatenate([w[e][0][:8], w[e][1][:8]], axis=0)
                acat[pl.ds(pl.multiple_of(i2 * 32 + e * 16, 16), 16), p * 128:(p + 1) * 128] = rows.astype(BF)
            for ra in range(2):
                rows = jnp.concatenate([w[0][ra][8:], w[1][ra][8:]], axis=0)
                at = pl.multiple_of(i2 * 16, 16)
                bb[ra, pl.ds(at, 16), p * 128:(p + 1) * 128] = jnp.where(real, rows, -rows).astype(BF)
                swapped = jnp.where(real, pltpu.roll(rows, 96, 1), pltpu.roll(rows, 32, 1))
                bb[ra, pl.ds(128 + at, 16), p * 128:(p + 1) * 128] = swapped.astype(BF)
        return carry

    lax.fori_loop(0, ns // 2, arrange, 0)
    for part in (s_buf.at[pl.ds(0, ns - 1)], s_buf.at[0, pl.ds(0, ny - 1)]):
        pltpu.make_async_copy(part, part, s_send).wait()

    prod = dot_nt(acat[...], bb[1 - c])
    psend[0] = prod[:, :128]
    psend[1] = prod[:, 128:]
    pair = pltpu.make_async_remote_copy(
        src_ref=psend, dst_ref=precv, send_sem=p_sem.at[0], recv_sem=p_sem.at[1],
        device_id={"src": me, "xl": m * 2 + 1 - c}, device_id_type=MESH)
    pair.start()
    prod = dot_nt(acat[...], bb[c])
    cown[0] = prod[:, :128]
    cown[1] = prod[:, 128:]
    pair.wait()

    for z in range(2):
        ck[pl.ds(z * 256, 256), :] = cown[z] + precv[z]

    halves = []
    for z in range(2):
        v = jnp.concatenate([ck[pl.ds(z * 256 + sp, 16, stride=16), :] for sp in range(16)], axis=0)
        for b in range(4):
            step = 8 << b
            v = v.reshape(8 >> b, 2, 16 << b, 128)
            low, high = v[:, 0].reshape(128, 128), v[:, 1].reshape(128, 128)
            keep = lane_bit((128, 128), b + 3)
            new_low = jnp.where(keep, low, pltpu.roll(high, step, 1))
            new_high = jnp.where(keep, pltpu.roll(low, 128 - step, 1), high)
            parts = (8 >> b, 1, 16 << b, 128)
            v = jnp.concatenate([new_low.reshape(parts), new_high.reshape(parts)], axis=1).reshape(256, 128)
        halves.append(v.reshape(16, 16, 128))
    d_buf[...] = jnp.concatenate(halves, axis=1).astype(BF)

    def c1(k, to, frm):
        return pltpu.make_async_remote_copy(
            src_ref=d_buf.at[to], dst_ref=e_buf.at[frm], send_sem=c1_send.at[k], recv_sem=c1_recv.at[k],
            device_id={"src": me, "xl": to * 2 + c}, device_id_type=MESH)

    def c1_go(k, carry):
        c1(k, (m + k) % nm, m).start()
        return carry

    def c1_wait(k, carry):
        c1(k, (m + k) % nm, (m + nm - k) % nm).wait()
        return carry

    lax.fori_loop(1, nm, c1_go, 0)
    e_buf[m] = d_buf[m]
    lax.fori_loop(1, nm, c1_wait, 0)

    for y in range(ny):
        tile = e_buf[2 * y].astype(F32) + e_buf[2 * y + 1].astype(F32)
        t_buf[pl.ds(y, 16, stride=16), :] = tile[:16]
        t_buf[pl.ds(8 + y, 16, stride=16), :] = tile[16:]
    h_buf[...] = t_buf[...].reshape(16, 16, 128).astype(BF)

    def c2(k, to, frm):
        return pltpu.make_async_remote_copy(
            src_ref=h_buf.at[to], dst_ref=g_buf.at[frm], send_sem=c2_send.at[k], recv_sem=c2_recv.at[k],
            device_id={"src": to, "xl": j}, device_id_type=MESH)

    def c2_go(k, carry):
        c2(k, (me + k) % ns, me).start()
        return carry

    def c2_wait(k, carry):
        c2(k, (me + k) % ns, (me + ns - k) % ns).wait()
        return carry

    lax.fori_loop(1, ns, c2_go, 0)
    g_buf[me] = h_buf[me]
    lax.fori_loop(1, ns, c2_wait, 0)

    got = g_buf[...].astype(F32)
    for z in range(2):
        flat = got[:, z * 8:(z + 1) * 8, :].reshape(F, 128)
        turned = flat.T * scale
        for s in range(16):
            sp = (s >> 1 & 1) * 8 + (s >> 2) * 2 + (s & 1)
            out_ref[s, :, z * F:(z + 1) * F] = turned[sp * 8:(sp + 1) * 8]


def per_device(ns, nx, src_traces, rec_traces):
    ny = nx // Q
    s, x, samples = src_traces.shape
    r = rec_traces.shape[1]
    scale = 1.0 / math.sqrt(x * nx)
    high, low = fourier_parts(samples)
    rows = s * x
    rec = rec_traces.reshape(rows, samples)
    out_shape = jax.ShapeDtypeStruct((s, r * ns // nx, 2 * F), F32)
    dma = pltpu.SemaphoreType.DMA
    nm = 2 * ny
    any_spec = pl.BlockSpec(memory_space=pl.ANY)
    return pl.pallas_call(
        functools.partial(kernel, ns, ny, scale),
        out_shape=out_shape,
        in_specs=[any_spec] * 4,
        out_specs=pl.BlockSpec(memory_space=pltpu.VMEM),
        scratch_shapes=[
            pltpu.VMEM((rows, samples), F32),
            pltpu.VMEM((8, rows, 128), F32),
            pltpu.VMEM((2 * F, samples), BF),
            pltpu.VMEM((2 * F, samples), BF),
            pltpu.VMEM((2 * rows, samples), BF),
            pltpu.VMEM((2 * rows, samples), BF),
            pltpu.VMEM((F * 16, 128), F32),
            pltpu.VMEM((ns, ny, 16, 128), BF),
            pltpu.VMEM((ns, ny, 16, 128), BF),
            pltpu.VMEM((256, 512), BF),
            pltpu.VMEM((2, 256, 512), BF),
            pltpu.VMEM((2, 256, 128), F32),
            pltpu.VMEM((2, 256, 128), F32),
            pltpu.VMEM((2, 256, 128), F32),
            pltpu.VMEM((512, 128), F32),
            pltpu.VMEM((16, 32, 128), BF),
            pltpu.VMEM((16, 32, 128), BF),
            pltpu.VMEM((256, 128), F32),
            pltpu.VMEM((16, 16, 128), BF),
            pltpu.VMEM((16, 16, 128), BF),
            dma((11,)), dma, dma((ns,)), dma((2,)),
            dma((nm,)), dma((nm,)), dma((ns,)), dma((ns,)), pltpu.SemaphoreType.REGULAR,
        ],
        compiler_params=pltpu.CompilerParams(
            collective_id=0, has_side_effects=True, vmem_limit_bytes=56 << 20),
    )(src_traces.reshape(rows, samples), rec, jnp.asarray(high), jnp.asarray(low))


def solution(mesh):
    body = functools.partial(per_device, mesh.shape["src"], mesh.shape["xl"])
    return jax.shard_map(
        body,
        mesh=mesh,
        in_specs=(P("src", "xl", None), P("xl", "src", None)),
        out_specs=P("src", "xl", None),
        check_vma=False,
    )
```

```python
import functools
import math

import jax
import jax.numpy as jnp
import numpy as np
from jax import lax
from jax.experimental import pallas as pl
from jax.experimental.pallas import tpu as pltpu
from jax.sharding import PartitionSpec as P

F = 128
FBASE = 4
Q = 4
BF = jnp.bfloat16
F32 = jnp.float32
MESH = pl.DeviceIdType.MESH
NT = (((1,), (1,)), ((), ()))


def fourier_parts(samples):
    times = np.arange(samples, dtype=np.int64)
    bins = FBASE + np.arange(F, dtype=np.int64)
    angles = (bins[:, None] * times[None, :] % samples) * (2.0 * math.pi / samples)
    table = np.concatenate([np.cos(angles), -np.sin(angles)], axis=0) / math.sqrt(samples)
    table = table.astype(np.float32)
    high = table.astype(jnp.bfloat16)
    low = (table - high.astype(np.float32)).astype(jnp.bfloat16)
    return high, low


def dot_nt(a, b):
    return lax.dot_general(a, b, NT, preferred_element_type=F32)


def lane_bit(shape, bit):
    lanes = lax.broadcasted_iota(jnp.int32, shape, len(shape) - 1)
    return ((lanes >> bit) & 1) == 0


def kernel(ns, ny, scale, src_ref, rec_ref, thi_ref, tlo_ref, out_ref,
           xa, xb, th, tl, xh, xlo, u, s_buf, r2, acat, bb,
           psend, precv, cown, ck, d_buf, e_buf, t_buf, h_buf, g_buf,
           in_sem, s_send, s_recv, p_sem,
           c1_send, c1_recv, c2_send, c2_recv, ready):
    me = lax.axis_index("src")
    j = lax.axis_index("xl")
    my_y = j // Q
    q = j % Q
    m = j // 2
    c = j % 2
    hi = m % 2
    nm = 2 * ny

    def load(a, b, k):
        return pltpu.make_async_copy(a, b, in_sem.at[k])

    loads = [load(thi_ref, th, 0), load(tlo_ref, tl, 1), load(src_ref, xa, 2)]
    rec_loads = [load(rec_ref.at[:, pl.ds(t * 128, 128)], xb.at[t], 3 + t) for t in range(8)]
    for item in loads + rec_loads:
        item.start()

    barrier = pltpu.get_barrier_semaphore()

    def greet_src(k, carry):
        pl.semaphore_signal(barrier, inc=1, device_id={"src": (me + k) % ns, "xl": j}, device_id_type=MESH)
        return carry

    def greet_y(k, carry):
        pl.semaphore_signal(barrier, inc=1, device_id={"src": me, "xl": (my_y + k) % ny * Q + q}, device_id_type=MESH)
        return carry

    def row_ready(k, carry):
        pl.semaphore_signal(ready, inc=1, device_id={"src": (me + k) % ns, "xl": j}, device_id_type=MESH)
        return carry

    def greet_x(k, carry):
        pl.semaphore_signal(barrier, inc=1, device_id={"src": me, "xl": k * Q + (1 - hi) * 2 + c}, device_id_type=MESH)
        return carry

    lax.fori_loop(1, ns, greet_src, 0)
    lax.fori_loop(1, ny, greet_y, 0)
    lax.fori_loop(0, ny, greet_x, 0)
    pl.semaphore_signal(barrier, inc=1, device_id={"src": me, "xl": m * 2 + 1 - c}, device_id_type=MESH)

    for item in loads:
        item.wait()

    def split(rows, start):
        high = rows.astype(BF)
        xh[pl.ds(start, rows.shape[0]), :] = high
        xlo[pl.ds(start, rows.shape[0]), :] = (rows - high.astype(F32)).astype(BF)

    def split_a(k, carry):
        at = pl.multiple_of(k * 64, 64)
        split(xa[pl.ds(at, 64), :], at)
        return carry

    def split_b(r, carry):
        slot = (r % 8) // 2 * 4 + (r // 8) * 2 + r % 2
        rows = jnp.concatenate([xb[t, pl.ds(r, 32, stride=16), :] for t in range(8)], axis=1)
        split(rows, pl.multiple_of(512 + slot * 32, 32))
        return carry

    def transform(n, carry):
        at = pl.multiple_of(n * 256, 256)
        high = xh[pl.ds(at, 256), :]
        low = xlo[pl.ds(at, 256), :]
        spec = dot_nt(th[...], high) + dot_nt(th[...], low) + dot_nt(tl[...], high)
        mask = lane_bit((F, 128), 5)
        for t in range(2):
            re = spec[:F, t * 128:(t + 1) * 128]
            im = spec[F:, t * 128:(t + 1) * 128]
            row = (n // 2) * 8 + (n % 2) * 4 + 2 * t
            u[pl.ds(row, F, stride=16), :] = jnp.where(mask, re, pltpu.roll(im, 32, 1))
            u[pl.ds(row + 1, F, stride=16), :] = jnp.where(mask, pltpu.roll(re, 96, 1), im)
        return carry

    lax.fori_loop(0, 8, split_a, 0)
    pl.semaphore_wait(barrier, ns + 2 * ny - 1)
    lax.fori_loop(1, ns, row_ready, 0)
    lax.fori_loop(0, 2, transform, 0)
    for item in rec_loads:
        item.wait()
    lax.fori_loop(0, 16, split_b, 0)
    lax.fori_loop(2, 4, transform, 0)

    for k in range(ns):
        s_buf[k] = u[k * 128:(k + 1) * 128, :].astype(BF).reshape(8, 16, 128)

    z, x_lo = me // 2, me % 2
    sign = 1 - 2 * c

    def send(dz, t, x):
        dy = 4 + (t + 1) // 2 * (1 - t % 2 * 2)
        to = (z + sign * dz + ns) % (ns // 2) * 2 + (x_lo + x) % 2
        to_y = (my_y + sign * dy + ns) % ny
        pltpu.make_async_remote_copy(
            src_ref=s_buf.at[to, to_y], dst_ref=r2.at[me, my_y], send_sem=s_send, recv_sem=s_recv.at[me],
            device_id={"src": to, "xl": to_y * Q + q}, device_id_type=MESH).start()

    def one(dz, k, carry):
        send(dz, k // 2, 1 - k % 2)
        return carry

    def both(dz, k, carry):
        send(dz * (1 - k % 2 * 2), k // 4, k // 2 % 2)
        return carry

    pl.semaphore_wait(ready, ns - 1)
    lax.fori_loop(0, 16, functools.partial(one, 4), 0)
    for dz in (3, 2, 1):
        lax.fori_loop(0, 32, functools.partial(both, dz), 0)
    lax.fori_loop(0, 15, functools.partial(one, 0), 0)
    pltpu.make_async_copy(s_buf.at[me, my_y], r2.at[me, my_y], s_recv.at[me]).start()

    def arrange(i2):
        top = lane_bit((16, 128), 6)
        real = lane_bit((16, 128), 5)
        for e in range(2):
            pltpu.make_async_copy(r2.at[2 * i2 + e], r2.at[2 * i2 + e], s_recv.at[2 * i2 + e]).wait()
        for p in range(4):
            w = []
            for e in range(2):
                u0 = r2[2 * i2 + e, 2 * p].astype(F32)
                u1 = r2[2 * i2 + e, 2 * p + 1].astype(F32)
                w.append((jnp.where(top, u0, pltpu.roll(u1, 64, 1)), jnp.where(top, pltpu.roll(u0, 64, 1), u1)))
                rows = jnp.concatenate([w[e][0][:8], w[e][1][:8]], axis=0)
                acat[pl.ds(pl.multiple_of(i2 * 32 + e * 16, 16), 16), p * 128:(p + 1) * 128] = rows.astype(BF)
            for ra in range(2):
                rows = jnp.concatenate([w[0][ra][8:], w[1][ra][8:]], axis=0)
                at = pl.multiple_of(i2 * 16, 16)
                bb[ra, pl.ds(at, 16), p * 128:(p + 1) * 128] = jnp.where(real, rows, -rows).astype(BF)
                swapped = jnp.where(real, pltpu.roll(rows, 96, 1), pltpu.roll(rows, 32, 1))
                bb[ra, pl.ds(128 + at, 16), p * 128:(p + 1) * 128] = swapped.astype(BF)

    def arrange_next(k, carry):
        dz = 4 - (k + 1) // 2
        arrange((z - sign * dz * (k % 2 * 2 - 1) + ns) % (ns // 2))
        return carry

    lax.fori_loop(0, ns // 2, arrange_next, 0)
    for part in (s_buf.at[pl.ds(0, ns - 1)], s_buf.at[0, pl.ds(0, ny - 1)]):
        pltpu.make_async_copy(part, part, s_send).wait()

    prod = dot_nt(acat[...], bb[1 - c])
    psend[0] = prod[:, :128]
    psend[1] = prod[:, 128:]
    pair = pltpu.make_async_remote_copy(
        src_ref=psend, dst_ref=precv, send_sem=p_sem.at[0], recv_sem=p_sem.at[1],
        device_id={"src": me, "xl": m * 2 + 1 - c}, device_id_type=MESH)
    pair.start()
    prod = dot_nt(acat[...], bb[c])
    cown[0] = prod[:, :128]
    cown[1] = prod[:, 128:]
    pair.wait()

    for z in range(2):
        ck[pl.ds(z * 256, 256), :] = cown[z] + precv[z]

    halves = []
    for z in range(2):
        v = jnp.concatenate([ck[pl.ds(z * 256 + sp, 16, stride=16), :] for sp in range(16)], axis=0)
        for b in range(4):
            step = 8 << b
            v = v.reshape(8 >> b, 2, 16 << b, 128)
            low, high = v[:, 0].reshape(128, 128), v[:, 1].reshape(128, 128)
            keep = lane_bit((128, 128), b + 3)
            new_low = jnp.where(keep, low, pltpu.roll(high, step, 1))
            new_high = jnp.where(keep, pltpu.roll(low, 128 - step, 1), high)
            parts = (8 >> b, 1, 16 << b, 128)
            v = jnp.concatenate([new_low.reshape(parts), new_high.reshape(parts)], axis=1).reshape(256, 128)
        halves.append(v.reshape(16, 16, 128))
    d_buf[...] = jnp.concatenate(halves, axis=1).astype(BF)

    def c1(k, to, frm):
        return pltpu.make_async_remote_copy(
            src_ref=d_buf.at[to], dst_ref=e_buf.at[frm], send_sem=c1_send.at[k], recv_sem=c1_recv.at[k],
            device_id={"src": me, "xl": to * 2 + c}, device_id_type=MESH)

    def c1_go(k, carry):
        c1(k, (m + k) % nm, m).start()
        return carry

    def c1_wait(k, carry):
        c1(k, (m + k) % nm, (m + nm - k) % nm).wait()
        return carry

    lax.fori_loop(1, nm, c1_go, 0)
    e_buf[m] = d_buf[m]
    lax.fori_loop(1, nm, c1_wait, 0)

    for y in range(ny):
        tile = e_buf[2 * y].astype(F32) + e_buf[2 * y + 1].astype(F32)
        t_buf[pl.ds(y, 16, stride=16), :] = tile[:16]
        t_buf[pl.ds(8 + y, 16, stride=16), :] = tile[16:]
    h_buf[...] = t_buf[...].reshape(16, 16, 128).astype(BF)

    def c2(k, to, frm):
        return pltpu.make_async_remote_copy(
            src_ref=h_buf.at[to], dst_ref=g_buf.at[frm], send_sem=c2_send.at[k], recv_sem=c2_recv.at[k],
            device_id={"src": to, "xl": j}, device_id_type=MESH)

    def c2_go(k, carry):
        c2(k, (me + k) % ns, me).start()
        return carry

    def c2_wait(k, carry):
        c2(k, (me + k) % ns, (me + ns - k) % ns).wait()
        return carry

    lax.fori_loop(1, ns, c2_go, 0)
    g_buf[me] = h_buf[me]
    lax.fori_loop(1, ns, c2_wait, 0)

    got = g_buf[...].astype(F32)
    for z in range(2):
        flat = got[:, z * 8:(z + 1) * 8, :].reshape(F, 128)
        turned = flat.T * scale
        for s in range(16):
            sp = (s >> 1 & 1) * 8 + (s >> 2) * 2 + (s & 1)
            out_ref[s, :, z * F:(z + 1) * F] = turned[sp * 8:(sp + 1) * 8]


def per_device(ns, nx, src_traces, rec_traces):
    ny = nx // Q
    s, x, samples = src_traces.shape
    r = rec_traces.shape[1]
    scale = 1.0 / math.sqrt(x * nx)
    high, low = fourier_parts(samples)
    rows = s * x
    rec = rec_traces.reshape(rows, samples)
    out_shape = jax.ShapeDtypeStruct((s, r * ns // nx, 2 * F), F32)
    dma = pltpu.SemaphoreType.DMA
    nm = 2 * ny
    any_spec = pl.BlockSpec(memory_space=pl.ANY)
    return pl.pallas_call(
        functools.partial(kernel, ns, ny, scale),
        out_shape=out_shape,
        in_specs=[any_spec] * 4,
        out_specs=pl.BlockSpec(memory_space=pltpu.VMEM),
        scratch_shapes=[
            pltpu.VMEM((rows, samples), F32),
            pltpu.VMEM((8, rows, 128), F32),
            pltpu.VMEM((2 * F, samples), BF),
            pltpu.VMEM((2 * F, samples), BF),
            pltpu.VMEM((2 * rows, samples), BF),
            pltpu.VMEM((2 * rows, samples), BF),
            pltpu.VMEM((F * 16, 128), F32),
            pltpu.VMEM((ns, ny, 16, 128), BF),
            pltpu.VMEM((ns, ny, 16, 128), BF),
            pltpu.VMEM((256, 512), BF),
            pltpu.VMEM((2, 256, 512), BF),
            pltpu.VMEM((2, 256, 128), F32),
            pltpu.VMEM((2, 256, 128), F32),
            pltpu.VMEM((2, 256, 128), F32),
            pltpu.VMEM((512, 128), F32),
            pltpu.VMEM((16, 32, 128), BF),
            pltpu.VMEM((16, 32, 128), BF),
            pltpu.VMEM((256, 128), F32),
            pltpu.VMEM((16, 16, 128), BF),
            pltpu.VMEM((16, 16, 128), BF),
            dma((11,)), dma, dma((ns,)), dma((2,)),
            dma((nm,)), dma((nm,)), dma((ns,)), dma((ns,)), pltpu.SemaphoreType.REGULAR,
        ],
        compiler_params=pltpu.CompilerParams(
            collective_id=0, has_side_effects=True, vmem_limit_bytes=56 << 20),
    )(src_traces.reshape(rows, samples), rec, jnp.asarray(high), jnp.asarray(low))


def solution(mesh):
    body = functools.partial(per_device, mesh.shape["src"], mesh.shape["xl"])
    return jax.shard_map(
        body,
        mesh=mesh,
        in_specs=(P("src", "xl", None), P("xl", "src", None)),
        out_specs=P("src", "xl", None),
        check_vma=False,
    )
```

```python
import functools
import math

import jax
import jax.numpy as jnp
import numpy as np
from jax import lax
from jax.experimental import pallas as pl
from jax.experimental.pallas import tpu as pltpu
from jax.sharding import PartitionSpec as P

F = 128
FBASE = 4
Q = 4
BF = jnp.bfloat16
F32 = jnp.float32
MESH = pl.DeviceIdType.MESH
NT = (((1,), (1,)), ((), ()))


def fourier_parts(samples):
    times = np.arange(samples, dtype=np.int64)
    bins = FBASE + np.arange(F, dtype=np.int64)
    angles = (bins[:, None] * times[None, :] % samples) * (2.0 * math.pi / samples)
    table = np.concatenate([np.cos(angles), -np.sin(angles)], axis=0) / math.sqrt(samples)
    table = table.astype(np.float32)
    high = table.astype(jnp.bfloat16)
    low = (table - high.astype(np.float32)).astype(jnp.bfloat16)
    return high, low


def dot_nt(a, b):
    return lax.dot_general(a, b, NT, preferred_element_type=F32)


def far_first(count, t):
    return count // 2 + (t + 1) // 2 * (1 - t % 2 * 2)


def lane_bit(shape, bit):
    lanes = lax.broadcasted_iota(jnp.int32, shape, len(shape) - 1)
    return ((lanes >> bit) & 1) == 0


def kernel(ns, ny, scale, src_ref, rec_ref, thi_ref, tlo_ref, out_ref,
           xa, xb, th, tl, xh, xlo, u, s_buf, r2, acat, bb,
           psend, precv, cown, ck, d_buf, e_buf, t_buf, h_buf, g_buf,
           in_sem, s_send, s_recv, p_sem,
           c1_send, c1_recv, c2_send, c2_recv, ready):
    me = lax.axis_index("src")
    j = lax.axis_index("xl")
    my_y = j // Q
    q = j % Q
    m = j // 2
    c = j % 2
    hi = m % 2
    nm = 2 * ny

    def load(a, b, k):
        return pltpu.make_async_copy(a, b, in_sem.at[k])

    loads = [load(thi_ref, th, 0), load(tlo_ref, tl, 1), load(src_ref, xa, 2)]
    rec_loads = [load(rec_ref.at[:, pl.ds(t * 128, 128)], xb.at[t], 3 + t) for t in range(8)]
    for item in loads + rec_loads:
        item.start()

    barrier = pltpu.get_barrier_semaphore()

    def greet_src(k, carry):
        to = (me + far_first(ns, k)) % ns
        pl.semaphore_signal(barrier, inc=1, device_id={"src": to, "xl": j}, device_id_type=MESH)
        return carry

    def greet_y(k, carry):
        to = (my_y + far_first(ny, k)) % ny
        pl.semaphore_signal(barrier, inc=1, device_id={"src": me, "xl": to * Q + q}, device_id_type=MESH)
        return carry

    def row_ready(k, carry):
        pl.semaphore_signal(ready, inc=1, device_id={"src": (me + far_first(ns, k)) % ns, "xl": j}, device_id_type=MESH)
        return carry

    def greet_x(k, carry):
        to = (my_y + far_first(ny, k)) % ny
        pl.semaphore_signal(barrier, inc=1, device_id={"src": me, "xl": to * Q + (1 - hi) * 2 + c}, device_id_type=MESH)
        return carry

    lax.fori_loop(0, ns - 1, greet_src, 0)
    lax.fori_loop(0, ny, greet_x, 0)
    lax.fori_loop(0, ny - 1, greet_y, 0)
    pl.semaphore_signal(barrier, inc=1, device_id={"src": me, "xl": m * 2 + 1 - c}, device_id_type=MESH)

    for item in loads:
        item.wait()

    def split(rows, start):
        high = rows.astype(BF)
        xh[pl.ds(start, rows.shape[0]), :] = high
        xlo[pl.ds(start, rows.shape[0]), :] = (rows - high.astype(F32)).astype(BF)

    def split_a(k, carry):
        at = pl.multiple_of(k * 64, 64)
        split(xa[pl.ds(at, 64), :], at)
        return carry

    def split_b(r, carry):
        slot = (r % 8) // 2 * 4 + (r // 8) * 2 + r % 2
        rows = jnp.concatenate([xb[t, pl.ds(r, 32, stride=16), :] for t in range(8)], axis=1)
        split(rows, pl.multiple_of(512 + slot * 32, 32))
        return carry

    def transform(n, carry):
        at = pl.multiple_of(n * 256, 256)
        high = xh[pl.ds(at, 256), :]
        low = xlo[pl.ds(at, 256), :]
        spec = dot_nt(th[...], high) + dot_nt(th[...], low) + dot_nt(tl[...], high)
        mask = lane_bit((F, 128), 5)
        for t in range(2):
            re = spec[:F, t * 128:(t + 1) * 128]
            im = spec[F:, t * 128:(t + 1) * 128]
            row = (n // 2) * 8 + (n % 2) * 4 + 2 * t
            u[pl.ds(row, F, stride=16), :] = jnp.where(mask, re, pltpu.roll(im, 32, 1))
            u[pl.ds(row + 1, F, stride=16), :] = jnp.where(mask, pltpu.roll(re, 96, 1), im)
        return carry

    lax.fori_loop(0, 8, split_a, 0)
    pl.semaphore_wait(barrier, ns + 2 * ny - 1)
    lax.fori_loop(0, ns - 1, row_ready, 0)
    lax.fori_loop(0, 2, transform, 0)
    for item in rec_loads:
        item.wait()
    lax.fori_loop(0, 16, split_b, 0)
    lax.fori_loop(2, 4, transform, 0)

    for k in range(ns):
        s_buf[k] = u[k * 128:(k + 1) * 128, :].astype(BF).reshape(8, 16, 128)

    z, x_lo = me // 2, me % 2
    sign = 1 - 2 * c

    def send(dz, t, x):
        dy = 4 + (t + 1) // 2 * (1 - t % 2 * 2)
        to = (z + sign * dz + ns) % (ns // 2) * 2 + (x_lo + x) % 2
        to_y = (my_y + sign * dy + ns) % ny
        pltpu.make_async_remote_copy(
            src_ref=s_buf.at[to, to_y], dst_ref=r2.at[me, my_y], send_sem=s_send, recv_sem=s_recv.at[me],
            device_id={"src": to, "xl": to_y * Q + q}, device_id_type=MESH).start()

    def one(dz, k, carry):
        send(dz, k // 2, 1 - k % 2)
        return carry

    def both(dz, k, carry):
        send(dz * (1 - k % 2 * 2), k // 4, k // 2 % 2)
        return carry

    pl.semaphore_wait(ready, ns - 1)
    lax.fori_loop(0, 16, functools.partial(one, 4), 0)
    for dz in (3, 2, 1):
        lax.fori_loop(0, 32, functools.partial(both, dz), 0)
    lax.fori_loop(0, 15, functools.partial(one, 0), 0)
    pltpu.make_async_copy(s_buf.at[me, my_y], r2.at[me, my_y], s_recv.at[me]).start()

    def arrange(i2):
        top = lane_bit((16, 128), 6)
        real = lane_bit((16, 128), 5)
        for e in range(2):
            pltpu.make_async_copy(r2.at[2 * i2 + e], r2.at[2 * i2 + e], s_recv.at[2 * i2 + e]).wait()
        for p in range(4):
            w = []
            for e in range(2):
                u0 = r2[2 * i2 + e, 2 * p].astype(F32)
                u1 = r2[2 * i2 + e, 2 * p + 1].astype(F32)
                w.append((jnp.where(top, u0, pltpu.roll(u1, 64, 1)), jnp.where(top, pltpu.roll(u0, 64, 1), u1)))
                rows = jnp.concatenate([w[e][0][:8], w[e][1][:8]], axis=0)
                acat[pl.ds(pl.multiple_of(i2 * 32 + e * 16, 16), 16), p * 128:(p + 1) * 128] = rows.astype(BF)
            for ra in range(2):
                rows = jnp.concatenate([w[0][ra][8:], w[1][ra][8:]], axis=0)
                at = pl.multiple_of(i2 * 16, 16)
                bb[ra, pl.ds(at, 16), p * 128:(p + 1) * 128] = jnp.where(real, rows, -rows).astype(BF)
                swapped = jnp.where(real, pltpu.roll(rows, 96, 1), pltpu.roll(rows, 32, 1))
                bb[ra, pl.ds(128 + at, 16), p * 128:(p + 1) * 128] = swapped.astype(BF)

    def arrange_next(k, carry):
        dz = 4 - (k + 1) // 2
        arrange((z - sign * dz * (k % 2 * 2 - 1) + ns) % (ns // 2))
        return carry

    lax.fori_loop(0, ns // 2, arrange_next, 0)

    prod = dot_nt(acat[...], bb[1 - c])
    psend[0] = prod[:, :128]
    psend[1] = prod[:, 128:]
    pair = pltpu.make_async_remote_copy(
        src_ref=psend, dst_ref=precv, send_sem=p_sem.at[0], recv_sem=p_sem.at[1],
        device_id={"src": me, "xl": m * 2 + 1 - c}, device_id_type=MESH)
    pair.start()
    prod = dot_nt(acat[...], bb[c])
    cown[0] = prod[:, :128]
    cown[1] = prod[:, 128:]
    pair.wait()

    for z in range(2):
        ck[pl.ds(z * 256, 256), :] = cown[z] + precv[z]

    halves = []
    for z in range(2):
        v = jnp.concatenate([ck[pl.ds(z * 256 + sp, 16, stride=16), :] for sp in range(16)], axis=0)
        for b in range(4):
            step = 8 << b
            v = v.reshape(8 >> b, 2, 16 << b, 128)
            low, high = v[:, 0].reshape(128, 128), v[:, 1].reshape(128, 128)
            keep = lane_bit((128, 128), b + 3)
            new_low = jnp.where(keep, low, pltpu.roll(high, step, 1))
            new_high = jnp.where(keep, pltpu.roll(low, 128 - step, 1), high)
            parts = (8 >> b, 1, 16 << b, 128)
            v = jnp.concatenate([new_low.reshape(parts), new_high.reshape(parts)], axis=1).reshape(256, 128)
        halves.append(v.reshape(16, 16, 128))
    d_buf[...] = jnp.concatenate(halves, axis=1).astype(BF)

    def c1(k, to, frm):
        return pltpu.make_async_remote_copy(
            src_ref=d_buf.at[to], dst_ref=e_buf.at[frm], send_sem=c1_send.at[k], recv_sem=c1_recv.at[k],
            device_id={"src": me, "xl": to * 2 + c}, device_id_type=MESH)

    def c1_go(k, carry):
        d = far_first(nm, k)
        c1(d, (m + d) % nm, m).start()
        return carry

    def c1_wait(k, carry):
        c1(k, (m + k) % nm, (m + nm - k) % nm).wait()
        return carry

    lax.fori_loop(0, nm - 1, c1_go, 0)
    e_buf[m] = d_buf[m]
    lax.fori_loop(1, nm, c1_wait, 0)

    for y in range(ny):
        tile = e_buf[2 * y].astype(F32) + e_buf[2 * y + 1].astype(F32)
        t_buf[pl.ds(y, 16, stride=16), :] = tile[:16]
        t_buf[pl.ds(8 + y, 16, stride=16), :] = tile[16:]
    h_buf[...] = t_buf[...].reshape(16, 16, 128).astype(BF)

    def c2(k, to, frm):
        return pltpu.make_async_remote_copy(
            src_ref=h_buf.at[to], dst_ref=g_buf.at[frm], send_sem=c2_send.at[k], recv_sem=c2_recv.at[k],
            device_id={"src": to, "xl": j}, device_id_type=MESH)

    def c2_go(k, carry):
        d = far_first(ns, k)
        c2(d, (me + d) % ns, me).start()
        return carry

    def c2_wait(k, carry):
        c2(k, (me + k) % ns, (me + ns - k) % ns).wait()
        return carry

    lax.fori_loop(0, ns - 1, c2_go, 0)
    g_buf[me] = h_buf[me]
    lax.fori_loop(1, ns, c2_wait, 0)

    for part in (s_buf.at[pl.ds(0, ns - 1)], s_buf.at[0, pl.ds(0, ny - 1)]):
        pltpu.make_async_copy(part, part, s_send).wait()

    got = g_buf[...].astype(F32)
    for z in range(2):
        flat = got[:, z * 8:(z + 1) * 8, :].reshape(F, 128)
        turned = flat.T * scale
        for s in range(16):
            sp = (s >> 1 & 1) * 8 + (s >> 2) * 2 + (s & 1)
            out_ref[s, :, z * F:(z + 1) * F] = turned[sp * 8:(sp + 1) * 8]


def per_device(ns, nx, src_traces, rec_traces):
    ny = nx // Q
    s, x, samples = src_traces.shape
    r = rec_traces.shape[1]
    scale = 1.0 / math.sqrt(x * nx)
    high, low = fourier_parts(samples)
    rows = s * x
    rec = rec_traces.reshape(rows, samples)
    out_shape = jax.ShapeDtypeStruct((s, r * ns // nx, 2 * F), F32)
    dma = pltpu.SemaphoreType.DMA
    nm = 2 * ny
    any_spec = pl.BlockSpec(memory_space=pl.ANY)
    return pl.pallas_call(
        functools.partial(kernel, ns, ny, scale),
        out_shape=out_shape,
        in_specs=[any_spec] * 4,
        out_specs=pl.BlockSpec(memory_space=pltpu.VMEM),
        scratch_shapes=[
            pltpu.VMEM((rows, samples), F32),
            pltpu.VMEM((8, rows, 128), F32),
            pltpu.VMEM((2 * F, samples), BF),
            pltpu.VMEM((2 * F, samples), BF),
            pltpu.VMEM((2 * rows, samples), BF),
            pltpu.VMEM((2 * rows, samples), BF),
            pltpu.VMEM((F * 16, 128), F32),
            pltpu.VMEM((ns, ny, 16, 128), BF),
            pltpu.VMEM((ns, ny, 16, 128), BF),
            pltpu.VMEM((256, 512), BF),
            pltpu.VMEM((2, 256, 512), BF),
            pltpu.VMEM((2, 256, 128), F32),
            pltpu.VMEM((2, 256, 128), F32),
            pltpu.VMEM((2, 256, 128), F32),
            pltpu.VMEM((512, 128), F32),
            pltpu.VMEM((16, 32, 128), BF),
            pltpu.VMEM((16, 32, 128), BF),
            pltpu.VMEM((256, 128), F32),
            pltpu.VMEM((16, 16, 128), BF),
            pltpu.VMEM((16, 16, 128), BF),
            dma((11,)), dma, dma((ns,)), dma((2,)),
            dma((nm,)), dma((nm,)), dma((ns,)), dma((ns,)), pltpu.SemaphoreType.REGULAR,
        ],
        compiler_params=pltpu.CompilerParams(
            collective_id=0, has_side_effects=True, vmem_limit_bytes=56 << 20),
    )(src_traces.reshape(rows, samples), rec, jnp.asarray(high), jnp.asarray(low))


def solution(mesh):
    body = functools.partial(per_device, mesh.shape["src"], mesh.shape["xl"])
    return jax.shard_map(
        body,
        mesh=mesh,
        in_specs=(P("src", "xl", None), P("xl", "src", None)),
        out_specs=P("src", "xl", None),
        check_vma=False,
    )
```

```python
import functools
import math

import jax
import jax.numpy as jnp
import numpy as np
from jax import lax
from jax.experimental import pallas as pl
from jax.experimental.pallas import tpu as pltpu
from jax.sharding import PartitionSpec as P

F = 128
FBASE = 4
Q = 4
BF = jnp.bfloat16
F32 = jnp.float32
MESH = pl.DeviceIdType.MESH
NT = (((1,), (1,)), ((), ()))


def fourier_parts(samples):
    times = np.arange(samples, dtype=np.int64)
    bins = FBASE + np.arange(F, dtype=np.int64)
    angles = (bins[:, None] * times[None, :] % samples) * (2.0 * math.pi / samples)
    table = np.concatenate([np.cos(angles), -np.sin(angles)], axis=0) / math.sqrt(samples)
    table = table.astype(np.float32)
    high = table.astype(jnp.bfloat16)
    low = (table - high.astype(np.float32)).astype(jnp.bfloat16)
    return high, low


def dot_nt(a, b):
    return lax.dot_general(a, b, NT, preferred_element_type=F32)


def far_first(count, t):
    return count // 2 + (t + 1) // 2 * (1 - t % 2 * 2)


def lane_bit(shape, bit):
    lanes = lax.broadcasted_iota(jnp.int32, shape, len(shape) - 1)
    return ((lanes >> bit) & 1) == 0


def kernel(ns, ny, scale, src_ref, rec_ref, thi_ref, tlo_ref, out_ref,
           xa, xb, th, tl, xh, xlo, u, s_buf, r2, acat, bb,
           psend, precv, cown, ck, d_buf, e_buf, t_buf, h_buf, g_buf,
           in_sem, s_send, s_recv, p_sem,
           c1_send, c1_recv, c2_send, c2_recv, ready):
    me = lax.axis_index("src")
    j = lax.axis_index("xl")
    my_y = j // Q
    q = j % Q
    m = j // 2
    c = j % 2
    hi = m % 2
    nm = 2 * ny

    def load(a, b, k):
        return pltpu.make_async_copy(a, b, in_sem.at[k])

    loads = [load(thi_ref, th, 0), load(tlo_ref, tl, 1), load(src_ref, xa, 2)]
    rec_loads = [load(rec_ref.at[:, pl.ds(t * 128, 128)], xb.at[t], 3 + t) for t in range(8)]
    for item in loads + rec_loads:
        item.start()

    barrier = pltpu.get_barrier_semaphore()

    def greet_src(k, carry):
        to = (me + far_first(ns, k)) % ns
        pl.semaphore_signal(barrier, inc=1, device_id={"src": to, "xl": j}, device_id_type=MESH)
        return carry

    def greet_y(k, carry):
        to = (my_y + far_first(ny, k)) % ny
        pl.semaphore_signal(barrier, inc=1, device_id={"src": me, "xl": to * Q + q}, device_id_type=MESH)
        return carry

    def row_ready(k, carry):
        pl.semaphore_signal(ready, inc=1, device_id={"src": (me + far_first(ns, k)) % ns, "xl": j}, device_id_type=MESH)
        return carry

    def greet_x(k, carry):
        to = (my_y + far_first(ny, k)) % ny
        pl.semaphore_signal(barrier, inc=1, device_id={"src": me, "xl": to * Q + (1 - hi) * 2 + c}, device_id_type=MESH)
        return carry

    lax.fori_loop(0, ns - 1, greet_src, 0)
    lax.fori_loop(0, ny, greet_x, 0)
    lax.fori_loop(0, ny - 1, greet_y, 0)
    pl.semaphore_signal(barrier, inc=1, device_id={"src": me, "xl": m * 2 + 1 - c}, device_id_type=MESH)

    for item in loads:
        item.wait()

    def split(rows, start):
        high = rows.astype(BF)
        xh[pl.ds(start, rows.shape[0]), :] = high
        xlo[pl.ds(start, rows.shape[0]), :] = (rows - high.astype(F32)).astype(BF)

    def split_a(k, carry):
        at = pl.multiple_of(k * 64, 64)
        split(xa[pl.ds(at, 64), :], at)
        return carry

    def split_b(r, carry):
        slot = (r % 8) // 2 * 4 + (r // 8) * 2 + r % 2
        rows = jnp.concatenate([xb[t, pl.ds(r, 32, stride=16), :] for t in range(8)], axis=1)
        split(rows, pl.multiple_of(512 + slot * 32, 32))
        return carry

    def transform(n, carry):
        at = pl.multiple_of(n * 256, 256)
        high = xh[pl.ds(at, 256), :]
        low = xlo[pl.ds(at, 256), :]
        spec = dot_nt(th[...], high) + dot_nt(th[...], low) + dot_nt(tl[...], high)
        mask = lane_bit((F, 128), 5)
        for t in range(2):
            re = spec[:F, t * 128:(t + 1) * 128]
            im = spec[F:, t * 128:(t + 1) * 128]
            row = (n // 2) * 8 + (n % 2) * 4 + 2 * t
            u[pl.ds(row, F, stride=16), :] = jnp.where(mask, re, pltpu.roll(im, 32, 1))
            u[pl.ds(row + 1, F, stride=16), :] = jnp.where(mask, pltpu.roll(re, 96, 1), im)
        return carry

    lax.fori_loop(0, 8, split_a, 0)
    lax.fori_loop(0, 2, transform, 0)
    pl.semaphore_wait(barrier, ns + 2 * ny - 1)
    lax.fori_loop(0, ns - 1, row_ready, 0)
    for item in rec_loads:
        item.wait()
    lax.fori_loop(0, 16, split_b, 0)
    lax.fori_loop(2, 4, transform, 0)

    for k in range(ns):
        s_buf[k] = u[k * 128:(k + 1) * 128, :].astype(BF).reshape(8, 16, 128)

    z, x_lo = me // 2, me % 2
    sign = 1 - 2 * c

    def send(dz, t, x):
        dy = 4 + (t + 1) // 2 * (1 - t % 2 * 2)
        to = (z + sign * dz + ns) % (ns // 2) * 2 + (x_lo + x) % 2
        to_y = (my_y + sign * dy + ns) % ny
        pltpu.make_async_remote_copy(
            src_ref=s_buf.at[to, to_y], dst_ref=r2.at[me, my_y], send_sem=s_send, recv_sem=s_recv.at[me],
            device_id={"src": to, "xl": to_y * Q + q}, device_id_type=MESH).start()

    def one(dz, k, carry):
        send(dz, k // 2, 1 - k % 2)
        return carry

    def both(dz, k, carry):
        send(dz * (1 - k % 2 * 2), k // 4, k // 2 % 2)
        return carry

    def in_column(dz, k, carry):
        send(dz * (1 - k % 2 * 2), ny - 1, k // 2 % 2)
        return carry

    def in_row(t, carry):
        send(0, t, 0)
        return carry

    def beside(t, carry):
        send(0, t, 1)
        return carry

    for k in range(2):
        send(4, ny - 1, k)
    for dz in (3, 2, 1):
        lax.fori_loop(0, 4, functools.partial(in_column, dz), 0)
    send(0, ny - 1, 1)
    lax.fori_loop(0, ny - 1, in_row, 0)
    pl.semaphore_wait(ready, ns - 1)
    lax.fori_loop(0, 14, functools.partial(one, 4), 0)
    for dz in (3, 2, 1):
        lax.fori_loop(0, 28, functools.partial(both, dz), 0)
    lax.fori_loop(0, ny - 1, beside, 0)
    pltpu.make_async_copy(s_buf.at[me, my_y], r2.at[me, my_y], s_recv.at[me]).start()

    def arrange(i2):
        top = lane_bit((16, 128), 6)
        real = lane_bit((16, 128), 5)
        for e in range(2):
            pltpu.make_async_copy(r2.at[2 * i2 + e], r2.at[2 * i2 + e], s_recv.at[2 * i2 + e]).wait()
        for p in range(4):
            w = []
            for e in range(2):
                u0 = r2[2 * i2 + e, 2 * p].astype(F32)
                u1 = r2[2 * i2 + e, 2 * p + 1].astype(F32)
                w.append((jnp.where(top, u0, pltpu.roll(u1, 64, 1)), jnp.where(top, pltpu.roll(u0, 64, 1), u1)))
                rows = jnp.concatenate([w[e][0][:8], w[e][1][:8]], axis=0)
                acat[pl.ds(pl.multiple_of(i2 * 32 + e * 16, 16), 16), p * 128:(p + 1) * 128] = rows.astype(BF)
            for ra in range(2):
                rows = jnp.concatenate([w[0][ra][8:], w[1][ra][8:]], axis=0)
                at = pl.multiple_of(i2 * 16, 16)
                bb[ra, pl.ds(at, 16), p * 128:(p + 1) * 128] = jnp.where(real, rows, -rows).astype(BF)
                swapped = jnp.where(real, pltpu.roll(rows, 96, 1), pltpu.roll(rows, 32, 1))
                bb[ra, pl.ds(128 + at, 16), p * 128:(p + 1) * 128] = swapped.astype(BF)

    def arrange_next(k, carry):
        dz = 4 - (k + 1) // 2
        arrange((z - sign * dz * (k % 2 * 2 - 1) + ns) % (ns // 2))
        return carry

    lax.fori_loop(0, ns // 2, arrange_next, 0)

    prod = dot_nt(acat[...], bb[1 - c])
    psend[0] = prod[:, :128]
    psend[1] = prod[:, 128:]
    pair = pltpu.make_async_remote_copy(
        src_ref=psend, dst_ref=precv, send_sem=p_sem.at[0], recv_sem=p_sem.at[1],
        device_id={"src": me, "xl": m * 2 + 1 - c}, device_id_type=MESH)
    pair.start()
    prod = dot_nt(acat[...], bb[c])
    cown[0] = prod[:, :128]
    cown[1] = prod[:, 128:]
    pair.wait()

    for z in range(2):
        ck[pl.ds(z * 256, 256), :] = cown[z] + precv[z]

    halves = []
    for z in range(2):
        v = jnp.concatenate([ck[pl.ds(z * 256 + sp, 16, stride=16), :] for sp in range(16)], axis=0)
        for b in range(4):
            step = 8 << b
            v = v.reshape(8 >> b, 2, 16 << b, 128)
            low, high = v[:, 0].reshape(128, 128), v[:, 1].reshape(128, 128)
            keep = lane_bit((128, 128), b + 3)
            new_low = jnp.where(keep, low, pltpu.roll(high, step, 1))
            new_high = jnp.where(keep, pltpu.roll(low, 128 - step, 1), high)
            parts = (8 >> b, 1, 16 << b, 128)
            v = jnp.concatenate([new_low.reshape(parts), new_high.reshape(parts)], axis=1).reshape(256, 128)
        halves.append(v.reshape(16, 16, 128))
    d_buf[...] = jnp.concatenate(halves, axis=1).astype(BF)

    def c1(k, to, frm):
        return pltpu.make_async_remote_copy(
            src_ref=d_buf.at[to], dst_ref=e_buf.at[frm], send_sem=c1_send.at[k], recv_sem=c1_recv.at[k],
            device_id={"src": me, "xl": to * 2 + c}, device_id_type=MESH)

    def c1_go(k, carry):
        d = far_first(nm, k)
        c1(d, (m + d) % nm, m).start()
        return carry

    def c1_wait(k, carry):
        c1(k, (m + k) % nm, (m + nm - k) % nm).wait()
        return carry

    lax.fori_loop(0, nm - 1, c1_go, 0)
    e_buf[m] = d_buf[m]
    lax.fori_loop(1, nm, c1_wait, 0)

    for y in range(ny):
        tile = e_buf[2 * y].astype(F32) + e_buf[2 * y + 1].astype(F32)
        t_buf[pl.ds(y, 16, stride=16), :] = tile[:16]
        t_buf[pl.ds(8 + y, 16, stride=16), :] = tile[16:]
    h_buf[...] = t_buf[...].reshape(16, 16, 128).astype(BF)

    def c2(k, to, frm):
        return pltpu.make_async_remote_copy(
            src_ref=h_buf.at[to], dst_ref=g_buf.at[frm], send_sem=c2_send.at[k], recv_sem=c2_recv.at[k],
            device_id={"src": to, "xl": j}, device_id_type=MESH)

    def c2_go(k, carry):
        d = far_first(ns, k)
        c2(d, (me + d) % ns, me).start()
        return carry

    def c2_wait(k, carry):
        c2(k, (me + k) % ns, (me + ns - k) % ns).wait()
        return carry

    lax.fori_loop(0, ns - 1, c2_go, 0)
    g_buf[me] = h_buf[me]
    lax.fori_loop(1, ns, c2_wait, 0)

    for part in (s_buf.at[pl.ds(0, ns - 1)], s_buf.at[0, pl.ds(0, ny - 1)]):
        pltpu.make_async_copy(part, part, s_send).wait()

    got = g_buf[...].astype(F32)
    for z in range(2):
        flat = got[:, z * 8:(z + 1) * 8, :].reshape(F, 128)
        turned = flat.T * scale
        for s in range(16):
            sp = (s >> 1 & 1) * 8 + (s >> 2) * 2 + (s & 1)
            out_ref[s, :, z * F:(z + 1) * F] = turned[sp * 8:(sp + 1) * 8]


def per_device(ns, nx, src_traces, rec_traces):
    ny = nx // Q
    s, x, samples = src_traces.shape
    r = rec_traces.shape[1]
    scale = 1.0 / math.sqrt(x * nx)
    high, low = fourier_parts(samples)
    rows = s * x
    rec = rec_traces.reshape(rows, samples)
    out_shape = jax.ShapeDtypeStruct((s, r * ns // nx, 2 * F), F32)
    dma = pltpu.SemaphoreType.DMA
    nm = 2 * ny
    any_spec = pl.BlockSpec(memory_space=pl.ANY)
    return pl.pallas_call(
        functools.partial(kernel, ns, ny, scale),
        out_shape=out_shape,
        in_specs=[any_spec] * 4,
        out_specs=pl.BlockSpec(memory_space=pltpu.VMEM),
        scratch_shapes=[
            pltpu.VMEM((rows, samples), F32),
            pltpu.VMEM((8, rows, 128), F32),
            pltpu.VMEM((2 * F, samples), BF),
            pltpu.VMEM((2 * F, samples), BF),
            pltpu.VMEM((2 * rows, samples), BF),
            pltpu.VMEM((2 * rows, samples), BF),
            pltpu.VMEM((F * 16, 128), F32),
            pltpu.VMEM((ns, ny, 16, 128), BF),
            pltpu.VMEM((ns, ny, 16, 128), BF),
            pltpu.VMEM((256, 512), BF),
            pltpu.VMEM((2, 256, 512), BF),
            pltpu.VMEM((2, 256, 128), F32),
            pltpu.VMEM((2, 256, 128), F32),
            pltpu.VMEM((2, 256, 128), F32),
            pltpu.VMEM((512, 128), F32),
            pltpu.VMEM((16, 32, 128), BF),
            pltpu.VMEM((16, 32, 128), BF),
            pltpu.VMEM((256, 128), F32),
            pltpu.VMEM((16, 16, 128), BF),
            pltpu.VMEM((16, 16, 128), BF),
            dma((11,)), dma, dma((ns,)), dma((2,)),
            dma((nm,)), dma((nm,)), dma((ns,)), dma((ns,)), pltpu.SemaphoreType.REGULAR,
        ],
        compiler_params=pltpu.CompilerParams(
            collective_id=0, has_side_effects=True, vmem_limit_bytes=56 << 20),
    )(src_traces.reshape(rows, samples), rec, jnp.asarray(high), jnp.asarray(low))


def solution(mesh):
    body = functools.partial(per_device, mesh.shape["src"], mesh.shape["xl"])
    return jax.shard_map(
        body,
        mesh=mesh,
        in_specs=(P("src", "xl", None), P("xl", "src", None)),
        out_specs=P("src", "xl", None),
        check_vma=False,
    )
```

```python
import functools
import math

import jax
import jax.numpy as jnp
import numpy as np
from jax import lax
from jax.experimental import pallas as pl
from jax.experimental.pallas import tpu as pltpu
from jax.sharding import PartitionSpec as P

F = 128
FBASE = 4
Q = 4
BF = jnp.bfloat16
F32 = jnp.float32
MESH = pl.DeviceIdType.MESH
NT = (((1,), (1,)), ((), ()))


def fourier_parts(samples):
    times = np.arange(samples, dtype=np.int64)
    bins = FBASE + np.arange(F, dtype=np.int64)
    angles = (bins[:, None] * times[None, :] % samples) * (2.0 * math.pi / samples)
    table = np.concatenate([np.cos(angles), -np.sin(angles)], axis=0) / math.sqrt(samples)
    table = table.astype(np.float32)
    high = table.astype(jnp.bfloat16)
    low = (table - high.astype(np.float32)).astype(jnp.bfloat16)
    return high, low


def dot_nt(a, b):
    return lax.dot_general(a, b, NT, preferred_element_type=F32)


def far_first(count, t):
    return count // 2 + (t + 1) // 2 * (1 - t % 2 * 2)


def lane_bit(shape, bit):
    lanes = lax.broadcasted_iota(jnp.int32, shape, len(shape) - 1)
    return ((lanes >> bit) & 1) == 0


def kernel(ns, ny, scale, src_ref, rec_ref, thi_ref, tlo_ref, out_ref,
           xa, xb, th, tl, xh, xlo, u, s_buf, r2, acat, bb,
           psend, precv, cown, ck, d_buf, e_buf, t_buf, h_buf, g_buf,
           in_sem, s_send, s_recv, p_sem,
           c1_send, c1_recv, c2_send, c2_recv, ready):
    me = lax.axis_index("src")
    j = lax.axis_index("xl")
    my_y = j // Q
    q = j % Q
    m = j // 2
    c = j % 2
    hi = m % 2
    nm = 2 * ny

    def load(a, b, k):
        return pltpu.make_async_copy(a, b, in_sem.at[k])

    loads = [load(thi_ref, th, 0), load(tlo_ref, tl, 1), load(src_ref, xa, 2)]
    rec_loads = [load(rec_ref.at[:, pl.ds(t * 128, 128)], xb.at[t], 3 + t) for t in range(8)]
    for item in loads + rec_loads:
        item.start()

    barrier = pltpu.get_barrier_semaphore()

    def greet_src(k, carry):
        to = (me + far_first(ns, k)) % ns
        pl.semaphore_signal(barrier, inc=1, device_id={"src": to, "xl": j}, device_id_type=MESH)
        return carry

    def greet_y(k, carry):
        to = (my_y + far_first(ny, k)) % ny
        pl.semaphore_signal(barrier, inc=1, device_id={"src": me, "xl": to * Q + q}, device_id_type=MESH)
        return carry

    def row_ready(k, carry):
        pl.semaphore_signal(ready, inc=1, device_id={"src": (me + far_first(ns, k)) % ns, "xl": j}, device_id_type=MESH)
        return carry

    def greet_x(k, carry):
        to = (my_y + far_first(ny, k)) % ny
        pl.semaphore_signal(barrier, inc=1, device_id={"src": me, "xl": to * Q + (1 - hi) * 2 + c}, device_id_type=MESH)
        return carry

    lax.fori_loop(0, ns - 1, greet_src, 0)
    lax.fori_loop(0, ny, greet_x, 0)
    lax.fori_loop(0, ny - 1, greet_y, 0)
    pl.semaphore_signal(barrier, inc=1, device_id={"src": me, "xl": m * 2 + 1 - c}, device_id_type=MESH)

    for item in loads:
        item.wait()

    def split(rows, start):
        high = rows.astype(BF)
        xh[pl.ds(start, rows.shape[0]), :] = high
        xlo[pl.ds(start, rows.shape[0]), :] = (rows - high.astype(F32)).astype(BF)

    def split_a(k, carry):
        at = pl.multiple_of(k * 64, 64)
        split(xa[pl.ds(at, 64), :], at)
        return carry

    def split_b(r, carry):
        slot = (r % 8) // 2 * 4 + (r // 8) * 2 + r % 2
        rows = jnp.concatenate([xb[t, pl.ds(r, 32, stride=16), :] for t in range(8)], axis=1)
        split(rows, pl.multiple_of(512 + slot * 32, 32))
        return carry

    def transform(n, carry):
        at = pl.multiple_of(n * 256, 256)
        high = xh[pl.ds(at, 256), :]
        low = xlo[pl.ds(at, 256), :]
        spec = dot_nt(th[...], high) + dot_nt(th[...], low) + dot_nt(tl[...], high)
        mask = lane_bit((F, 128), 5)
        for t in range(2):
            re = spec[:F, t * 128:(t + 1) * 128]
            im = spec[F:, t * 128:(t + 1) * 128]
            row = (n // 2) * 8 + (n % 2) * 4 + 2 * t
            u[pl.ds(row, F, stride=16), :] = jnp.where(mask, re, pltpu.roll(im, 32, 1))
            u[pl.ds(row + 1, F, stride=16), :] = jnp.where(mask, pltpu.roll(re, 96, 1), im)
        return carry

    lax.fori_loop(0, 8, split_a, 0)
    lax.fori_loop(0, 2, transform, 0)
    for item in rec_loads:
        item.wait()
    lax.fori_loop(0, 16, split_b, 0)
    pl.semaphore_wait(barrier, ns + 2 * ny - 1)
    lax.fori_loop(0, ns - 1, row_ready, 0)
    lax.fori_loop(2, 4, transform, 0)

    for k in range(ns):
        s_buf[k] = u[k * 128:(k + 1) * 128, :].astype(BF).reshape(8, 16, 128)

    z, x_lo = me // 2, me % 2
    sign = 1 - 2 * c

    def send(dz, t, x):
        dy = 4 + (t + 1) // 2 * (1 - t % 2 * 2)
        to = (z + sign * dz + ns) % (ns // 2) * 2 + (x_lo + x) % 2
        to_y = (my_y + sign * dy + ns) % ny
        pltpu.make_async_remote_copy(
            src_ref=s_buf.at[to, to_y], dst_ref=r2.at[me, my_y], send_sem=s_send, recv_sem=s_recv.at[me],
            device_id={"src": to, "xl": to_y * Q + q}, device_id_type=MESH).start()

    def one(dz, k, carry):
        send(dz, k // 2, 1 - k % 2)
        return carry

    def both(dz, k, carry):
        send(dz * (1 - k % 2 * 2), k // 4, k // 2 % 2)
        return carry

    def in_column(dz, k, carry):
        send(dz * (1 - k % 2 * 2), ny - 1, k // 2 % 2)
        return carry

    def in_row(t, carry):
        send(0, t, 0)
        return carry

    def beside(t, carry):
        send(0, t, 1)
        return carry

    for k in range(2):
        send(4, ny - 1, k)
    for dz in (3, 2, 1):
        lax.fori_loop(0, 4, functools.partial(in_column, dz), 0)
    send(0, ny - 1, 1)
    lax.fori_loop(0, ny - 1, in_row, 0)
    pl.semaphore_wait(ready, ns - 1)
    lax.fori_loop(0, 14, functools.partial(one, 4), 0)
    for dz in (3, 2, 1):
        lax.fori_loop(0, 28, functools.partial(both, dz), 0)
    lax.fori_loop(0, ny - 1, beside, 0)
    pltpu.make_async_copy(s_buf.at[me, my_y], r2.at[me, my_y], s_recv.at[me]).start()

    def arrange(i2):
        top = lane_bit((16, 128), 6)
        real = lane_bit((16, 128), 5)
        for e in range(2):
            pltpu.make_async_copy(r2.at[2 * i2 + e], r2.at[2 * i2 + e], s_recv.at[2 * i2 + e]).wait()
        for p in range(4):
            w = []
            for e in range(2):
                u0 = r2[2 * i2 + e, 2 * p].astype(F32)
                u1 = r2[2 * i2 + e, 2 * p + 1].astype(F32)
                w.append((jnp.where(top, u0, pltpu.roll(u1, 64, 1)), jnp.where(top, pltpu.roll(u0, 64, 1), u1)))
                rows = jnp.concatenate([w[e][0][:8], w[e][1][:8]], axis=0)
                acat[pl.ds(pl.multiple_of(i2 * 32 + e * 16, 16), 16), p * 128:(p + 1) * 128] = rows.astype(BF)
            for ra in range(2):
                rows = jnp.concatenate([w[0][ra][8:], w[1][ra][8:]], axis=0)
                at = pl.multiple_of(i2 * 16, 16)
                bb[ra, pl.ds(at, 16), p * 128:(p + 1) * 128] = jnp.where(real, rows, -rows).astype(BF)
                swapped = jnp.where(real, pltpu.roll(rows, 96, 1), pltpu.roll(rows, 32, 1))
                bb[ra, pl.ds(128 + at, 16), p * 128:(p + 1) * 128] = swapped.astype(BF)

    def arrange_next(k, carry):
        dz = 4 - (k + 1) // 2
        arrange((z - sign * dz * (k % 2 * 2 - 1) + ns) % (ns // 2))
        return carry

    lax.fori_loop(0, ns // 2, arrange_next, 0)

    prod = dot_nt(acat[...], bb[1 - c])
    psend[0] = prod[:, :128]
    psend[1] = prod[:, 128:]
    pair = pltpu.make_async_remote_copy(
        src_ref=psend, dst_ref=precv, send_sem=p_sem.at[0], recv_sem=p_sem.at[1],
        device_id={"src": me, "xl": m * 2 + 1 - c}, device_id_type=MESH)
    pair.start()
    prod = dot_nt(acat[...], bb[c])
    cown[0] = prod[:, :128]
    cown[1] = prod[:, 128:]
    pair.wait()

    for z in range(2):
        ck[pl.ds(z * 256, 256), :] = cown[z] + precv[z]

    halves = []
    for z in range(2):
        v = jnp.concatenate([ck[pl.ds(z * 256 + sp, 16, stride=16), :] for sp in range(16)], axis=0)
        for b in range(4):
            step = 8 << b
            v = v.reshape(8 >> b, 2, 16 << b, 128)
            low, high = v[:, 0].reshape(128, 128), v[:, 1].reshape(128, 128)
            keep = lane_bit((128, 128), b + 3)
            new_low = jnp.where(keep, low, pltpu.roll(high, step, 1))
            new_high = jnp.where(keep, pltpu.roll(low, 128 - step, 1), high)
            parts = (8 >> b, 1, 16 << b, 128)
            v = jnp.concatenate([new_low.reshape(parts), new_high.reshape(parts)], axis=1).reshape(256, 128)
        halves.append(v.reshape(16, 16, 128))
    d_buf[...] = jnp.concatenate(halves, axis=1).astype(BF)

    def c1(k, to, frm):
        return pltpu.make_async_remote_copy(
            src_ref=d_buf.at[to], dst_ref=e_buf.at[frm], send_sem=c1_send.at[k], recv_sem=c1_recv.at[k],
            device_id={"src": me, "xl": to * 2 + c}, device_id_type=MESH)

    def c1_go(k, carry):
        d = far_first(nm, k)
        c1(d, (m + d) % nm, m).start()
        return carry

    def c1_wait(k, carry):
        c1(k, (m + k) % nm, (m + nm - k) % nm).wait()
        return carry

    lax.fori_loop(0, nm - 1, c1_go, 0)
    e_buf[m] = d_buf[m]
    lax.fori_loop(1, nm, c1_wait, 0)

    for y in range(ny):
        tile = e_buf[2 * y].astype(F32) + e_buf[2 * y + 1].astype(F32)
        t_buf[pl.ds(y, 16, stride=16), :] = tile[:16]
        t_buf[pl.ds(8 + y, 16, stride=16), :] = tile[16:]
    h_buf[...] = t_buf[...].reshape(16, 16, 128).astype(BF)

    def c2(k, to, frm):
        return pltpu.make_async_remote_copy(
            src_ref=h_buf.at[to], dst_ref=g_buf.at[frm], send_sem=c2_send.at[k], recv_sem=c2_recv.at[k],
            device_id={"src": to, "xl": j}, device_id_type=MESH)

    def c2_go(k, carry):
        d = far_first(ns, k)
        c2(d, (me + d) % ns, me).start()
        return carry

    def c2_wait(k, carry):
        c2(k, (me + k) % ns, (me + ns - k) % ns).wait()
        return carry

    lax.fori_loop(0, ns - 1, c2_go, 0)
    g_buf[me] = h_buf[me]
    lax.fori_loop(1, ns, c2_wait, 0)

    for part in (s_buf.at[pl.ds(0, ns - 1)], s_buf.at[0, pl.ds(0, ny - 1)]):
        pltpu.make_async_copy(part, part, s_send).wait()

    got = g_buf[...].astype(F32)
    for z in range(2):
        flat = got[:, z * 8:(z + 1) * 8, :].reshape(F, 128)
        turned = flat.T * scale
        for s in range(16):
            sp = (s >> 1 & 1) * 8 + (s >> 2) * 2 + (s & 1)
            out_ref[s, :, z * F:(z + 1) * F] = turned[sp * 8:(sp + 1) * 8]


def per_device(ns, nx, src_traces, rec_traces):
    ny = nx // Q
    s, x, samples = src_traces.shape
    r = rec_traces.shape[1]
    scale = 1.0 / math.sqrt(x * nx)
    high, low = fourier_parts(samples)
    rows = s * x
    rec = rec_traces.reshape(rows, samples)
    out_shape = jax.ShapeDtypeStruct((s, r * ns // nx, 2 * F), F32)
    dma = pltpu.SemaphoreType.DMA
    nm = 2 * ny
    any_spec = pl.BlockSpec(memory_space=pl.ANY)
    return pl.pallas_call(
        functools.partial(kernel, ns, ny, scale),
        out_shape=out_shape,
        in_specs=[any_spec] * 4,
        out_specs=pl.BlockSpec(memory_space=pltpu.VMEM),
        scratch_shapes=[
            pltpu.VMEM((rows, samples), F32),
            pltpu.VMEM((8, rows, 128), F32),
            pltpu.VMEM((2 * F, samples), BF),
            pltpu.VMEM((2 * F, samples), BF),
            pltpu.VMEM((2 * rows, samples), BF),
            pltpu.VMEM((2 * rows, samples), BF),
            pltpu.VMEM((F * 16, 128), F32),
            pltpu.VMEM((ns, ny, 16, 128), BF),
            pltpu.VMEM((ns, ny, 16, 128), BF),
            pltpu.VMEM((256, 512), BF),
            pltpu.VMEM((2, 256, 512), BF),
            pltpu.VMEM((2, 256, 128), F32),
            pltpu.VMEM((2, 256, 128), F32),
            pltpu.VMEM((2, 256, 128), F32),
            pltpu.VMEM((512, 128), F32),
            pltpu.VMEM((16, 32, 128), BF),
            pltpu.VMEM((16, 32, 128), BF),
            pltpu.VMEM((256, 128), F32),
            pltpu.VMEM((16, 16, 128), BF),
            pltpu.VMEM((16, 16, 128), BF),
            dma((11,)), dma, dma((ns,)), dma((2,)),
            dma((nm,)), dma((nm,)), dma((ns,)), dma((ns,)), pltpu.SemaphoreType.REGULAR,
        ],
        compiler_params=pltpu.CompilerParams(
            collective_id=0, has_side_effects=True, vmem_limit_bytes=56 << 20),
    )(src_traces.reshape(rows, samples), rec, jnp.asarray(high), jnp.asarray(low))


def solution(mesh):
    body = functools.partial(per_device, mesh.shape["src"], mesh.shape["xl"])
    return jax.shard_map(
        body,
        mesh=mesh,
        in_specs=(P("src", "xl", None), P("xl", "src", None)),
        out_specs=P("src", "xl", None),
        check_vma=False,
    )
```
